256 devices in a mesh: samp: 8 (over x, z_hi), feat: 32 (over y, z_lo, core).
Axes of the slice: x: 4, y: 4, z: 8 (z_hi: 2, z_lo: 4; z = z_hi * 4 + z_lo), core: 2. Of those that a mesh axis runs over, the one named last changes fastest.
Arguments:
- embeddings: bfloat16 [8192, 1024], P('samp'), may hold values from -6 to 6
- frequencies: bfloat16 [1024, 8192], P(None, 'feat'), may hold values from -0.1875 to 0.1875
- phases: float32 [8192], P('feat'), may hold values from -3.140625 to 3.140625
- treat_freq: float32 [8192], P('feat'), may hold values from -3.140625 to 3.140625
- treatment: int32 [8192], P('samp'), may hold values from 0 to 1
- flips: int32 [8192], P('samp'), may hold values from 0 to 1
- panel: int32 [1], replicated, may hold values from 0 to 15
Outputs:
- schur: float32 [8192, 8192], P('samp', 'feat')
- panel_factor: float32 [8192, 512], P('samp')
- moment_scaled: float32 [8192], P('feat')
The draws below stay inside these ranges and needn't reach their ends.
All inputs are finite; a program needn't handle non-finite values.
Results may differ from the reference program's by a relative error of at most 0.0032.
Values may be sent and summed in bfloat16 or wider, within the bound.
No kernel may reach another device: no remote copies, remote signals or barrier semaphores. Data moves between devices by JAX's collectives and lax.ppermute only.
A program may use at most 128 MiB of HBM per device.

```python
import jax
import jax.numpy as jnp
from jax import lax

EMB = 1024
FEATS = 8192
PANEL = 512
IMPS = 8192


def plant(array, own_key, smallest, top_value):
    shape = array.shape
    index_at = [jax.random.randint(jax.random.fold_in(own_key, axis), (), 0, shape[axis]) for axis in range(len(shape))]
    array = array.at[tuple(index_at)].set(smallest)
    longest = shape.index(max(shape))
    index_at[longest] = (index_at[longest] + 1) % shape[longest]
    return array.at[tuple(index_at)].set(top_value)


def level_of(own_key, shape, shards, least, high):
    def one(axis_at, blocks):
        steps = jax.random.uniform(jax.random.fold_in(jax.random.fold_in(own_key, 6), axis_at), (blocks,), jnp.float32, least / len(shards), high / len(shards))
        return jnp.repeat(jnp.exp(steps), shape[axis_at] // blocks).reshape((-1,) + (1,) * (len(shape) - axis_at - 1))

    gain = one(*shards[0])
    for cut in shards[1:]:
        gain = gain * one(*cut)
    return gain


def normal_values(own_key, shape, spread, bound, cuts=(), held_as=jnp.bfloat16):
    level = level_of(own_key, shape, cuts, -0.22, 0.18) if cuts else 1.0
    array = jax.random.normal(own_key, shape, jnp.float32) * spread * level
    return jnp.minimum(jnp.maximum(array, -bound), bound).astype(held_as)


def setup_inputs(seed: int = 0) -> dict:
    key_of = jax.random.split(jax.random.key(seed), 8)
    embeddings = normal_values(key_of[0], (IMPS, EMB), 1.0, 6.0, ((0, 8),))
    frequencies = normal_values(key_of[1], (EMB, FEATS), EMB ** -0.5, 0.1875, ((1, 32),))
    phases = jnp.clip(jax.random.uniform(key_of[2], (FEATS,), jnp.float32, -3.140625, 3.140625), -3.140625, 3.140625)
    treat_freq = jnp.clip(jax.random.uniform(key_of[3], (FEATS,), jnp.float32, -3.140625, 3.140625), -3.140625, 3.140625)
    treatment = plant(jax.random.randint(key_of[4], (IMPS,), 0, 2), jax.random.fold_in(key_of[4], 1), 0, 1).astype(jnp.int32)
    flips = plant(jax.random.randint(key_of[5], (IMPS,), 0, 2), jax.random.fold_in(key_of[5], 1), 0, 1).astype(jnp.int32)
    panel = jax.random.randint(key_of[6], (1,), 0, FEATS // PANEL).astype(jnp.int32)
    return {"embeddings": embeddings, "frequencies": frequencies, "phases": phases, "treat_freq": treat_freq, "treatment": treatment, "flips": flips, "panel": panel}


ridge = 0.1
root_two = 1.4142135623730951

def cosine_map(project, phases, treat_freq, treated):
    return root_two * jnp.cos(project + phases[None, :] + treated[:, None] * treat_freq[None, :])

def reference(embeddings, frequencies, phases, treat_freq, treatment, flips, panel):
    project = jnp.dot(embeddings.astype(jnp.float32), frequencies.astype(jnp.float32), preferred_element_type=jnp.float32)
    treated = treatment.astype(jnp.float32)
    flipped = flips.astype(jnp.float32)
    counter = treated + flipped - 2.0 * treated * flipped
    observed = cosine_map(project, phases, treat_freq, treated)
    counterfactual = cosine_map(project, phases, treat_freq, counter)
    features = observed.astype(jnp.bfloat16).astype(jnp.float32)
    sample_count = embeddings.shape[0]
    gram = jnp.dot(features.T.astype(jnp.float32), features.astype(jnp.float32), precision=lax.Precision.HIGHEST, preferred_element_type=jnp.float32) / sample_count
    gram = gram + ridge * jnp.eye(FEATS, dtype=jnp.float32)
    moment = lax.optimization_barrier(jnp.sum(counterfactual - observed, axis=0)) / sample_count
    first_col = (panel[0] * PANEL).astype(jnp.int32)
    panel_cols = lax.dynamic_slice_in_dim(gram, first_col, PANEL, 1)
    pivot = lax.dynamic_slice_in_dim(panel_cols, first_col, PANEL, 0)
    lower = jnp.linalg.cholesky(pivot)
    factor_t = lax.linalg.triangular_solve(lower, panel_cols.T, left_side=True, lower=True)
    panel_factor = factor_t.T
    schur = gram - jnp.dot(panel_factor, factor_t, precision=lax.Precision.HIGHEST)
    moment_panel = lax.dynamic_slice_in_dim(moment, first_col, PANEL, 0)
    solved = lax.linalg.triangular_solve(lower, moment_panel[:, None], left_side=True, lower=True)[:, 0]
    reduced = moment - jnp.dot(panel_factor, solved, precision=lax.Precision.HIGHEST)
    return (schur, panel_factor, jnp.sqrt(jnp.float32(sample_count)) * reduced)
```

```python
import jax
import jax.numpy as jnp
from jax import lax
from jax.experimental import pallas as pl
from jax.experimental.pallas import tpu as pltpu
from jax.sharding import Mesh
from jax.sharding import PartitionSpec as P

PANEL = 512
ridge = 0.1
f32 = jnp.float32
bf16 = jnp.bfloat16
HIGHEST = lax.Precision.HIGHEST

SAMP = ("x", "zh")
FEAT = ("y", "zl", "core")

SINE = (
    -8.885765875337938,
    58.46599556065702,
    -115.4071939365197,
    108.47536728137668,
    -59.39695452559278,
    20.275610646954046,
)


def cosine(x):
    turns = x * 0.15915494309189535
    s = jnp.abs(turns - jnp.round(turns)) - 0.25
    u = s * s
    p = SINE[5]
    for c in SINE[4::-1]:
        p = p * u + c
    return s * p


def dot(left, right, dims, **kw):
    return lax.dot_general(left, right, (dims, ((), ())), preferred_element_type=f32, **kw)


def gram_body(zh_ref, all_ref, near_ref, far_ref, own_ref, panel_ref, pivot_ref):
    step = pl.program_id(0)
    imps = near_ref.shape[1]
    width = near_ref.shape[2]
    blocks = all_ref.shape[2]
    row_blocks = blocks - PANEL // width

    @pl.when(step == 0)
    def _():
        own_ref[...] = jnp.zeros_like(own_ref)
        panel_ref[...] = jnp.zeros_like(panel_ref)
        pivot_ref[...] = jnp.zeros_like(pivot_ref)

    mine = jnp.where(step % 2 == zh_ref[0], near_ref[0], far_ref[0])
    block = [all_ref[:, 0, b].reshape(imps, width) for b in range(blocks)]
    elim = jnp.concatenate(block[row_blocks:], axis=1)
    mine_t = mine.T
    elim_t = elim.T
    for b in range(blocks):
        at = slice(b * width, (b + 1) * width)
        own_ref[:, at] += dot(mine_t, block[b], ((1,), (0,)))
        if b < row_blocks:
            panel_ref[:, at] += dot(elim_t, block[b], ((1,), (0,)))
    pivot_ref[...] += dot(elim_t, elim, ((1,), (0,)))


def gram_sums(zh, gathered, near, far):
    feat, samp, blocks, piece, width = gathered.shape
    imps = near.shape[1]
    rows = blocks * width - PANEL
    return pl.pallas_call(
        gram_body,
        out_shape=(
            jax.ShapeDtypeStruct((width, blocks * width), f32),
            jax.ShapeDtypeStruct((PANEL, rows), f32),
            jax.ShapeDtypeStruct((PANEL, PANEL), f32),
        ),
        grid_spec=pltpu.PrefetchScalarGridSpec(
            num_scalar_prefetch=1,
            grid=(samp,),
            in_specs=[
                pl.BlockSpec(
                    (feat, 1, blocks, piece, width),
                    lambda i, zh_ref: (0, i, 0, 0, 0),
                ),
                pl.BlockSpec((1, imps, width), lambda i, zh_ref: (i // 2, 0, 0)),
                pl.BlockSpec((1, imps, width), lambda i, zh_ref: (i // 2, 0, 0)),
            ],
            out_specs=[
                pl.BlockSpec((width, blocks * width), lambda i, zh_ref: (0, 0)),
                pl.BlockSpec((PANEL, rows), lambda i, zh_ref: (0, 0)),
                pl.BlockSpec((PANEL, PANEL), lambda i, zh_ref: (0, 0)),
            ],
        ),
        compiler_params=pltpu.CompilerParams(vmem_limit_bytes=50 << 20),
        name="gram_sums",
    )(zh, gathered, near, far)


def invert_body(a_ref, out_ref, work, diag):
    n = a_ref.shape[0]
    nb = 128
    work[:, :n] = a_ref[...]
    row = lax.broadcasted_iota(jnp.int32, (n, n), 0)
    col = lax.broadcasted_iota(jnp.int32, (n, n), 1)
    work[:, n:] = (row == col).astype(f32)
    sub = lax.broadcasted_iota(jnp.int32, (8, nb), 0)
    lane = lax.broadcasted_iota(jnp.int32, (8, nb), 1)
    eye = (
        lax.broadcasted_iota(jnp.int32, (nb, nb), 0) == lax.broadcasted_iota(jnp.int32, (nb, nb), 1)
    ).astype(f32)
    for lo in range(0, n, nb):
        hi = lo + nb
        diag[:, :nb] = work[lo:hi, lo:hi]
        diag[:, nb:] = eye
        for q in range(0, nb, 8):
            ra = diag[q : q + 8, :nb]
            rb = diag[q : q + 8, nb:]
            cols = [jnp.broadcast_to(ra[:, q + c : q + c + 1], (8, nb)) for c in range(8)]
            pivots = jnp.ones((8, nb), f32)
            for c in range(8):
                d = jnp.broadcast_to(cols[c][c : c + 1, :], (8, nb))
                pivots = jnp.where(sub == c, d, pivots)
                if c < 7:
                    mult = jnp.where(sub > c, cols[c] / d, 0.0)
                    for e in range(c + 1, 8):
                        cols[e] = cols[e] - mult * jnp.broadcast_to(cols[e][c : c + 1, :], (8, nb))
                    ra = ra - mult * jnp.broadcast_to(ra[c : c + 1, :], (8, nb))
                    rb = rb - mult * jnp.broadcast_to(rb[c : c + 1, :], (8, nb))
            scale = lax.rsqrt(pivots)
            ra = ra * scale
            rb = rb * scale
            diag[q : q + 8, nb:] = rb
            if q + 8 < nb:
                low = jnp.where(lane >= q + 8, ra, 0.0)
                update = dot(low, jnp.concatenate([low, rb], 1), ((0,), (0,)), precision=HIGHEST)
                diag[q + 8 :, :] = diag[q + 8 :, :] - update[q + 8 :, :]
        upper = dot(diag[:, nb:], work[lo:hi, hi : n + hi], ((1,), (0,)), precision=HIGHEST)
        rest = n - hi
        out_ref[lo:hi, :hi] = upper[:, rest:]
        if rest:
            work[hi:, hi : n + hi] = work[hi:, hi : n + hi] - dot(
                upper[:, :rest], upper, ((0,), (0,)), precision=HIGHEST
            )
            out_ref[lo:hi, hi:] = jnp.zeros((nb, rest), f32)


def inverse_factor(pivot):
    n = pivot.shape[0]
    return pl.pallas_call(
        invert_body,
        out_shape=jax.ShapeDtypeStruct((n, n), f32),
        scratch_shapes=[pltpu.VMEM((n, 2 * n), f32), pltpu.VMEM((128, 256), f32)],
        compiler_params=pltpu.CompilerParams(vmem_limit_bytes=32 << 20),
        name="inverse_factor",
    )(pivot)


def finish_body(count, at_ref, own_ref, panel_ref, inv_ref, m_ref, mk_ref, schur_ref, factor_ref, red_ref):
    row0, col0, first = at_ref[0], at_ref[1], at_ref[2]
    scale = 1.0 / count
    rows = panel_ref.shape[1]
    width = own_ref.shape[0]

    def diagonal(shape, r0, c0):
        r = r0 + lax.broadcasted_iota(jnp.int32, shape, 0)
        c = c0 + lax.broadcasted_iota(jnp.int32, shape, 1)
        return jnp.where(r == c, ridge, 0.0)

    inv = inv_ref[...]
    panel = panel_ref[...].T * scale + diagonal((rows, PANEL), row0, first)
    factor = dot(panel, inv, ((1,), (1,)), precision=HIGHEST)
    factor_ref[...] = factor
    cross = own_ref[:, rows:] * scale + diagonal((width, PANEL), col0, first)
    cross = dot(cross, inv, ((1,), (1,)), precision=HIGHEST)
    gram = own_ref[:, :rows].T * scale + diagonal((rows, width), row0, col0)
    schur_ref[...] = gram - dot(factor, cross, ((1,), (1,)), precision=HIGHEST)
    solved = dot(mk_ref[...], inv, ((1,), (1,)), precision=HIGHEST)
    reduced = m_ref[...] - dot(solved, cross, ((1,), (1,)), precision=HIGHEST)
    red_ref[...] = reduced * (count**0.5)


def finish(count, at, own, panel, inv, m, mk):
    width = own.shape[0]
    rows = panel.shape[1]
    vmem = pl.BlockSpec(memory_space=pltpu.VMEM)
    return pl.pallas_call(
        lambda *refs: finish_body(count, *refs),
        out_shape=(
            jax.ShapeDtypeStruct((rows, width), f32),
            jax.ShapeDtypeStruct((rows, PANEL), f32),
            jax.ShapeDtypeStruct((1, width), f32),
        ),
        in_specs=[pl.BlockSpec(memory_space=pltpu.SMEM)] + [vmem] * 5,
        out_specs=[vmem] * 3,
        compiler_params=pltpu.CompilerParams(vmem_limit_bytes=50 << 20),
        name="finish",
    )(at, own, panel, inv, m, mk)


def per_device(embeddings, frequencies, phases, treat_freq, treatment, flips, panel):
    imps = embeddings.shape[0]
    width = frequencies.shape[1]
    samp = lax.axis_size(SAMP)
    feat = lax.axis_size(FEAT)
    samp_index = lax.axis_index(SAMP)
    feat_index = lax.axis_index(FEAT)
    count = imps * samp
    rows = width * feat // samp
    piece = imps // feat
    elim = PANEL // width

    project = jnp.dot(embeddings, frequencies, preferred_element_type=f32)
    treated = treatment.astype(f32)
    flipped = flips.astype(f32)
    counter = treated + flipped - 2.0 * treated * flipped
    base = project + phases[None, :]
    observed = cosine(base + treated[:, None] * treat_freq[None, :])
    counterfactual = cosine(base + counter[:, None] * treat_freq[None, :])
    moment_part = jnp.sum(counterfactual - observed, axis=0)
    feature = observed.astype(bf16)

    swapped = lax.ppermute(feature, "zh", [(0, 1), (1, 0)])
    near = lax.all_gather(feature, "x")
    far = lax.all_gather(swapped, "x")

    shares = lax.all_to_all(
        feature.reshape(feat, piece, width), FEAT, split_axis=0, concat_axis=0, tiled=True
    )
    first_dev = panel[0] * elim
    picked = lax.dynamic_slice_in_dim(shares, first_dev, elim, 0)
    send = jnp.concatenate(
        [
            shares.reshape(samp, feat // samp, piece, width),
            jnp.broadcast_to(picked[None], (samp, elim, piece, width)),
        ],
        axis=1,
    )
    share = lax.all_to_all(send, SAMP, split_axis=0, concat_axis=0, tiled=True)
    gathered = lax.all_gather(share, FEAT)

    share, moment_part = lax.optimization_barrier((share, moment_part))
    moment = lax.psum(moment_part, SAMP) / count
    moments = lax.all_gather(lax.all_gather(moment, ("zl", "core")), "y").reshape(-1)
    moment_panel = lax.dynamic_slice_in_dim(moments, panel[0] * PANEL, PANEL, 0)

    zh = lax.axis_index("zh").astype(jnp.int32)[None]
    own, panel_sum, pivot_sum = gram_sums(zh, gathered, near, far)
    pivot = pivot_sum / count + ridge * jnp.eye(PANEL, dtype=f32)
    inv = inverse_factor(pivot)
    at = jnp.stack([samp_index * rows, feat_index * width, panel[0] * PANEL]).astype(jnp.int32)
    schur, factor, reduced = finish(
        count, at, own, panel_sum, inv, moment[None], moment_panel[None]
    )
    return (schur, factor, reduced[0])


def solution(mesh):
    fine = Mesh(mesh.devices.reshape(4, 2, 4, 4, 2), ("x", "zh", "y", "zl", "core"))
    return jax.shard_map(
        per_device,
        mesh=fine,
        in_specs=(P(SAMP, None), P(None, FEAT), P(FEAT), P(FEAT), P(SAMP), P(SAMP), P()),
        out_specs=(P(SAMP, FEAT), P(SAMP, None), P(FEAT)),
        check_vma=False,
    )
```

```python
import jax
import jax.numpy as jnp
from jax import lax
from jax.experimental import pallas as pl
from jax.experimental.pallas import tpu as pltpu
from jax.sharding import Mesh
from jax.sharding import PartitionSpec as P

PANEL = 512
ridge = 0.1
f32 = jnp.float32
bf16 = jnp.bfloat16
HIGHEST = lax.Precision.HIGHEST

SAMP = ("x", "zh")
FEAT = ("y", "zl", "core")

SINE = (
    -8.885765875337938,
    58.46599556065702,
    -115.4071939365197,
    108.47536728137668,
    -59.39695452559278,
    20.275610646954046,
)


def cosine(x):
    turns = x * 0.15915494309189535
    s = jnp.abs(turns - jnp.round(turns)) - 0.25
    u = s * s
    p = SINE[5]
    for c in SINE[4::-1]:
        p = p * u + c
    return s * p


def dot(left, right, dims, **kw):
    return lax.dot_general(left, right, (dims, ((), ())), preferred_element_type=f32, **kw)


def split(a):
    high = a.astype(bf16)
    return high, (a - high.astype(f32)).astype(bf16)


def dot3(left, right, dims):
    lh, ll = left
    rh, rl = right
    return dot(lh, rh, dims) + (dot(lh, rl, dims) + dot(ll, rh, dims))


NT = ((1,), (1,))


def gram_body(
    count, at_ref, all_ref, near_ref, far_ref, inv_ref, schur_ref, factor_ref, red_ref, own, panel, mom
):
    step = pl.program_id(0)
    imps = near_ref.shape[1]
    width = near_ref.shape[2]
    feat = all_ref.shape[0]
    piece = imps // feat
    rows = panel.shape[1]
    row_blocks = rows // width
    blocks = row_blocks + PANEL // width

    @pl.when(step == 0)
    def _():
        own[...] = jnp.zeros_like(own)
        panel[...] = jnp.zeros_like(panel)
        mom[...] = jnp.zeros_like(mom)

    mine = jnp.where(step % 2 == at_ref[3], near_ref[0], far_ref[0])
    block = [
        all_ref[:, 0, b * piece : (b + 1) * piece, :].reshape(imps, width) for b in range(blocks)
    ]
    mine_t = mine.T
    elim_t = jnp.concatenate(block[row_blocks:], axis=1).T
    for b in range(blocks):
        at = slice(b * width, (b + 1) * width)
        own[:, at] += dot(mine_t, block[b], ((1,), (0,)))
        if b < row_blocks:
            panel[:, at] += dot(elim_t, block[b], ((1,), (0,)))
    mom[...] += jnp.sum(all_ref[:, 0, blocks * piece :, :].astype(f32), axis=1)

    @pl.when(step == pl.num_programs(0) - 1)
    def _():
        row0, col0, first = at_ref[0], at_ref[1], at_ref[2]
        scale = 1.0 / count

        def diagonal(shape, r0, c0):
            r = r0 + lax.broadcasted_iota(jnp.int32, shape, 0)
            c = c0 + lax.broadcasted_iota(jnp.int32, shape, 1)
            return jnp.where(r == c, ridge, 0.0)

        inv = split(inv_ref[...])
        cross = own[:, rows:] * scale + diagonal((width, PANEL), col0, first)
        cross = dot3(split(cross), inv, NT)
        cross_parts = split(cross)
        for lo in range(0, rows, width):
            at = slice(lo, lo + width)
            cols = panel[:, at].T * scale + diagonal((width, PANEL), row0 + lo, first)
            factor = dot3(split(cols), inv, NT)
            factor_ref[at, :] = factor
            gram = own[:, at].T * scale + diagonal((width, width), row0 + lo, col0)
            schur_ref[at, :] = gram - dot3(split(factor), cross_parts, NT)
        own_dev = at_ref[4]
        first_dev = at_ref[5]
        picked = [mom[pl.ds(first_dev + k, 1), :] * scale for k in range(PANEL // width)]
        elim = jnp.broadcast_to(jnp.concatenate(picked, axis=1), (8, PANEL))
        solved = dot(elim, inv_ref[...], NT, precision=HIGHEST)
        part = dot(solved, cross, NT, precision=HIGHEST)
        reduced = mom[pl.ds(own_dev, 1), :] * scale - part[:1]
        red_ref[...] = reduced * (count**0.5)


def gram_schur(count, at, gathered, near, far, inv):
    feat, samp, held, width = gathered.shape
    imps = near.shape[1]
    rows = width * feat // samp
    fixed = lambda i, at_ref: (0, 0)
    return pl.pallas_call(
        lambda *refs: gram_body(count, *refs),
        out_shape=(
            jax.ShapeDtypeStruct((rows, width), f32),
            jax.ShapeDtypeStruct((rows, PANEL), f32),
            jax.ShapeDtypeStruct((1, width), f32),
        ),
        grid_spec=pltpu.PrefetchScalarGridSpec(
            num_scalar_prefetch=1,
            grid=(samp,),
            in_specs=[
                pl.BlockSpec((feat, 1, held, width), lambda i, at_ref: (0, i, 0, 0)),
                pl.BlockSpec((1, imps, width), lambda i, at_ref: (i // 2, 0, 0)),
                pl.BlockSpec((1, imps, width), lambda i, at_ref: ((i // 2 - at_ref[6]) & 3, 0, 0)),
                pl.BlockSpec((PANEL, PANEL), fixed),
            ],
            out_specs=[
                pl.BlockSpec((rows, width), fixed),
                pl.BlockSpec((rows, PANEL), fixed),
                pl.BlockSpec((1, width), fixed),
            ],
            scratch_shapes=[
                pltpu.VMEM((width, rows + PANEL), f32),
                pltpu.VMEM((PANEL, rows), f32),
                pltpu.VMEM((feat, width), f32),
            ],
        ),
        compiler_params=pltpu.CompilerParams(vmem_limit_bytes=50 << 20),
        name="gram_schur",
    )(at, gathered, near, far, inv)


def invert_body(a_ref, out_ref, work, diag):
    n = a_ref.shape[0]
    nb = 128
    work[:, :n] = a_ref[...]
    row = lax.broadcasted_iota(jnp.int32, (n, n), 0)
    col = lax.broadcasted_iota(jnp.int32, (n, n), 1)
    work[:, n:] = (row == col).astype(f32)
    sub = lax.broadcasted_iota(jnp.int32, (8, nb), 0)
    lane = lax.broadcasted_iota(jnp.int32, (8, nb), 1)
    eye = (
        lax.broadcasted_iota(jnp.int32, (nb, nb), 0) == lax.broadcasted_iota(jnp.int32, (nb, nb), 1)
    ).astype(f32)
    for lo in range(0, n, nb):
        hi = lo + nb
        diag[:, :nb] = work[lo:hi, lo:hi]
        diag[:, nb:] = eye
        for q in range(0, nb, 8):
            ra = diag[q : q + 8, :nb]
            rb = diag[q : q + 8, nb:]
            cols = [jnp.broadcast_to(ra[:, q + c : q + c + 1], (8, nb)) for c in range(8)]
            pivots = jnp.ones((8, nb), f32)
            for c in range(8):
                d = jnp.broadcast_to(cols[c][c : c + 1, :], (8, nb))
                pivots = jnp.where(sub == c, d, pivots)
                if c < 7:
                    mult = jnp.where(sub > c, cols[c] / d, 0.0)
                    for e in range(c + 1, 8):
                        cols[e] = cols[e] - mult * jnp.broadcast_to(cols[e][c : c + 1, :], (8, nb))
                    ra = ra - mult * jnp.broadcast_to(ra[c : c + 1, :], (8, nb))
                    rb = rb - mult * jnp.broadcast_to(rb[c : c + 1, :], (8, nb))
            scale = lax.rsqrt(pivots)
            ra = ra * scale
            rb = rb * scale
            diag[q : q + 8, nb:] = rb
            if q + 8 < nb:
                low = jnp.where(lane >= q + 8, ra, 0.0)
                update = dot(low, jnp.concatenate([low, rb], 1), ((0,), (0,)), precision=HIGHEST)
                diag[q + 8 :, :] = diag[q + 8 :, :] - update[q + 8 :, :]
        upper = dot(diag[:, nb:], work[lo:hi, hi : n + hi], ((1,), (0,)), precision=HIGHEST)
        rest = n - hi
        out_ref[lo:hi, :hi] = upper[:, rest:]
        if rest:
            work[hi:, hi : n + hi] = work[hi:, hi : n + hi] - dot(
                upper[:, :rest], upper, ((0,), (0,)), precision=HIGHEST
            )
            out_ref[lo:hi, hi:] = jnp.zeros((nb, rest), f32)


def inverse_factor(pivot):
    n = pivot.shape[0]
    return pl.pallas_call(
        invert_body,
        out_shape=jax.ShapeDtypeStruct((n, n), f32),
        scratch_shapes=[pltpu.VMEM((n, 2 * n), f32), pltpu.VMEM((128, 256), f32)],
        compiler_params=pltpu.CompilerParams(vmem_limit_bytes=32 << 20),
        name="inverse_factor",
    )(pivot)


def per_device(embeddings, frequencies, phases, treat_freq, treatment, flips, panel):
    imps = embeddings.shape[0]
    width = frequencies.shape[1]
    samp = lax.axis_size(SAMP)
    feat = lax.axis_size(FEAT)
    samp_index = lax.axis_index(SAMP)
    feat_index = lax.axis_index(FEAT)
    count = imps * samp
    rows = width * feat // samp
    piece = imps // feat
    elim = PANEL // width

    project = jnp.dot(embeddings, frequencies, preferred_element_type=f32)
    treated = treatment.astype(f32)
    flipped = flips.astype(f32)
    counter = treated + flipped - 2.0 * treated * flipped
    base = project + phases[None, :]
    observed = cosine(base + treated[:, None] * treat_freq[None, :])
    counterfactual = cosine(base + counter[:, None] * treat_freq[None, :])
    moment_part = jnp.sum(counterfactual - observed, axis=0)
    feature = observed.astype(bf16)

    near = lax.all_gather(feature, "x")

    shares = lax.all_to_all(
        feature.reshape(feat, piece, width), FEAT, split_axis=0, concat_axis=0, tiled=True
    )
    first_dev = panel[0] * elim
    picked = lax.dynamic_slice_in_dim(shares, first_dev, elim, 0)
    high = lax.reduce_precision(moment_part, 8, 7)
    middle = lax.reduce_precision(moment_part - high, 8, 7)
    low = moment_part - high - middle
    moment_rows = jnp.pad(jnp.stack([high, middle, low]), ((0, 13), (0, 0))).astype(bf16)
    held = jnp.concatenate([picked.reshape(elim * piece, width), moment_rows], axis=0)
    send = jnp.concatenate(
        [
            shares.reshape(samp, feat // samp * piece, width),
            jnp.broadcast_to(held[None], (samp,) + held.shape),
        ],
        axis=1,
    )
    share = lax.all_to_all(send, SAMP, split_axis=0, concat_axis=0, tiled=True)
    gathered = lax.all_gather(share, FEAT)

    later, share = lax.optimization_barrier((feature, share))
    swapped = lax.ppermute(later, "zh", [(0, 1), (1, 0)])
    xs = lax.axis_size("x")
    far = jnp.stack(
        [swapped]
        + [lax.ppermute(swapped, "x", [(i, (i - r) % xs) for i in range(xs)]) for r in range(1, xs)]
    )

    skip = feat // samp * piece
    parts = [
        share[:, skip + k * piece : skip + (k + 1) * piece, :].reshape(samp * piece, width)
        for k in range(elim)
    ]
    mine = jnp.concatenate(parts, axis=1)
    partial = dot(mine, mine, ((0,), (0,)))
    slabs = lax.all_to_all(
        partial.reshape(feat, PANEL // feat, PANEL), FEAT, split_axis=0, concat_axis=0, tiled=True
    )
    slab = jnp.sum(slabs, axis=0)
    pivot = lax.all_to_all(
        jnp.broadcast_to(slab[None], slabs.shape), FEAT, split_axis=0, concat_axis=0, tiled=True
    ).reshape(PANEL, PANEL)
    inv = inverse_factor(pivot / count + ridge * jnp.eye(PANEL, dtype=f32))

    at = jnp.stack(
        [
            samp_index * rows,
            feat_index * width,
            panel[0] * PANEL,
            lax.axis_index("zh"),
            feat_index,
            first_dev,
            lax.axis_index("x"),
        ]
    ).astype(jnp.int32)
    schur, factor, reduced = gram_schur(count, at, gathered, near, far, inv)
    return (schur, factor, reduced[0])


def solution(mesh):
    fine = Mesh(mesh.devices.reshape(4, 2, 4, 4, 2), ("x", "zh", "y", "zl", "core"))
    return jax.shard_map(
        per_device,
        mesh=fine,
        in_specs=(P(SAMP, None), P(None, FEAT), P(FEAT), P(FEAT), P(SAMP), P(SAMP), P()),
        out_specs=(P(SAMP, FEAT), P(SAMP, None), P(FEAT)),
        check_vma=False,
    )
```

```python
import jax
import jax.numpy as jnp
from jax import lax
from jax.experimental import pallas as pl
from jax.experimental.pallas import tpu as pltpu
from jax.sharding import Mesh
from jax.sharding import PartitionSpec as P

PANEL = 512
ridge = 0.1
f32 = jnp.float32
bf16 = jnp.bfloat16
HIGHEST = lax.Precision.HIGHEST

SAMP = ("x", "zh")
FEAT = ("y", "zl", "core")

SINE = (
    -8.885765875337938,
    58.46599556065702,
    -115.4071939365197,
    108.47536728137668,
    -59.39695452559278,
    20.275610646954046,
)


def cosine(x):
    turns = x * 0.15915494309189535
    s = jnp.abs(turns - jnp.round(turns)) - 0.25
    u = s * s
    p = SINE[5]
    for c in SINE[4::-1]:
        p = p * u + c
    return s * p


def dot(left, right, dims, **kw):
    return lax.dot_general(left, right, (dims, ((), ())), preferred_element_type=f32, **kw)


def split(a):
    high = a.astype(bf16)
    return high, (a - high.astype(f32)).astype(bf16)


def dot3(left, right, dims):
    lh, ll = left
    rh, rl = right
    return dot(lh, rh, dims) + (dot(lh, rl, dims) + dot(ll, rh, dims))


NT = ((1,), (1,))


def invert(a, out_ref, work, diag):
    n = a.shape[0]
    nb = 128
    work[:, :n] = a
    row = lax.broadcasted_iota(jnp.int32, (n, n), 0)
    col = lax.broadcasted_iota(jnp.int32, (n, n), 1)
    work[:, n:] = (row == col).astype(f32)
    sub = lax.broadcasted_iota(jnp.int32, (8, nb), 0)
    lane = lax.broadcasted_iota(jnp.int32, (8, nb), 1)
    eye = (
        lax.broadcasted_iota(jnp.int32, (nb, nb), 0) == lax.broadcasted_iota(jnp.int32, (nb, nb), 1)
    ).astype(f32)
    for lo in range(0, n, nb):
        hi = lo + nb
        diag[:, :nb] = work[lo:hi, lo:hi]
        diag[:, nb:] = eye
        for q in range(0, nb, 8):
            ra = diag[q : q + 8, :nb]
            rb = diag[q : q + 8, nb:]
            cols = [jnp.broadcast_to(ra[:, q + c : q + c + 1], (8, nb)) for c in range(8)]
            pivots = jnp.ones((8, nb), f32)
            for c in range(8):
                d = jnp.broadcast_to(cols[c][c : c + 1, :], (8, nb))
                pivots = jnp.where(sub == c, d, pivots)
                if c < 7:
                    mult = jnp.where(sub > c, cols[c] / d, 0.0)
                    for e in range(c + 1, 8):
                        cols[e] = cols[e] - mult * jnp.broadcast_to(cols[e][c : c + 1, :], (8, nb))
                    ra = ra - mult * jnp.broadcast_to(ra[c : c + 1, :], (8, nb))
                    rb = rb - mult * jnp.broadcast_to(rb[c : c + 1, :], (8, nb))
            scale = lax.rsqrt(pivots)
            ra = ra * scale
            rb = rb * scale
            diag[q : q + 8, nb:] = rb
            if q + 8 < nb:
                low = jnp.where(lane >= q + 8, ra, 0.0)
                update = dot(low, jnp.concatenate([low, rb], 1), ((0,), (0,)), precision=HIGHEST)
                diag[q + 8 :, :] = diag[q + 8 :, :] - update[q + 8 :, :]
        upper = dot(diag[:, nb:], work[lo:hi, hi : n + hi], ((1,), (0,)), precision=HIGHEST)
        rest = n - hi
        out_ref[lo:hi, :hi] = upper[:, rest:]
        if rest:
            work[hi:, hi : n + hi] = work[hi:, hi : n + hi] - dot(
                upper[:, :rest], upper, ((0,), (0,)), precision=HIGHEST
            )
            out_ref[lo:hi, hi:] = jnp.zeros((nb, rest), f32)


def gram_body(
    count, at_ref, all_ref, near_ref, far_ref, schur_ref, factor_ref, red_ref,
    own, panel, pivot, mom, inv_ref, work, diag
):
    step = pl.program_id(0)
    imps = near_ref.shape[1]
    width = near_ref.shape[2]
    feat = all_ref.shape[0]
    piece = imps // feat
    rows = panel.shape[1]
    row_blocks = rows // width
    blocks = row_blocks + PANEL // width

    @pl.when(step == 0)
    def _():
        own[...] = jnp.zeros_like(own)
        panel[...] = jnp.zeros_like(panel)
        pivot[...] = jnp.zeros_like(pivot)
        mom[...] = jnp.zeros_like(mom)

    mine = jnp.where(step % 2 == at_ref[3], near_ref[0], far_ref[0])
    block = [
        all_ref[:, 0, b * piece : (b + 1) * piece, :].reshape(imps, width) for b in range(blocks)
    ]
    mine_t = mine.T
    elim = jnp.concatenate(block[row_blocks:], axis=1)
    elim_t = elim.T
    for b in range(blocks):
        at = slice(b * width, (b + 1) * width)
        own[:, at] += dot(mine_t, block[b], ((1,), (0,)))
        if b < row_blocks:
            panel[:, at] += dot(elim_t, block[b], ((1,), (0,)))
    pivot[...] += dot(elim_t, elim, ((1,), (0,)))
    mom[...] += jnp.sum(all_ref[:, 0, blocks * piece :, :].astype(f32), axis=1)

    @pl.when(step == pl.num_programs(0) - 1)
    def _():
        row0, col0, first = at_ref[0], at_ref[1], at_ref[2]
        scale = 1.0 / count

        def diagonal(shape, r0, c0):
            r = r0 + lax.broadcasted_iota(jnp.int32, shape, 0)
            c = c0 + lax.broadcasted_iota(jnp.int32, shape, 1)
            return jnp.where(r == c, ridge, 0.0)

        invert(pivot[...] * scale + diagonal((PANEL, PANEL), 0, 0), inv_ref, work, diag)
        inv = split(inv_ref[...])
        cross = own[:, rows:] * scale + diagonal((width, PANEL), col0, first)
        cross = dot3(split(cross), inv, NT)
        cross_parts = split(cross)
        for lo in range(0, rows, width):
            at = slice(lo, lo + width)
            cols = panel[:, at].T * scale + diagonal((width, PANEL), row0 + lo, first)
            factor = dot3(split(cols), inv, NT)
            factor_ref[at, :] = factor
            gram = own[:, at].T * scale + diagonal((width, width), row0 + lo, col0)
            schur_ref[at, :] = gram - dot3(split(factor), cross_parts, NT)
        own_dev = at_ref[4]
        first_dev = at_ref[5]
        picked = [mom[pl.ds(first_dev + k, 1), :] * scale for k in range(PANEL // width)]
        elim = jnp.broadcast_to(jnp.concatenate(picked, axis=1), (8, PANEL))
        solved = dot(elim, inv_ref[...], NT, precision=HIGHEST)
        part = dot(solved, cross, NT, precision=HIGHEST)
        reduced = mom[pl.ds(own_dev, 1), :] * scale - part[:1]
        red_ref[...] = reduced * (count**0.5)


def gram_schur(count, at, gathered, near, far):
    feat, samp, held, width = gathered.shape
    imps = near.shape[1]
    rows = width * feat // samp
    fixed = lambda i, at_ref: (0, 0)
    return pl.pallas_call(
        lambda *refs: gram_body(count, *refs),
        out_shape=(
            jax.ShapeDtypeStruct((rows, width), f32),
            jax.ShapeDtypeStruct((rows, PANEL), f32),
            jax.ShapeDtypeStruct((1, width), f32),
        ),
        grid_spec=pltpu.PrefetchScalarGridSpec(
            num_scalar_prefetch=1,
            grid=(samp,),
            in_specs=[
                pl.BlockSpec((feat, 1, held, width), lambda i, at_ref: (0, i, 0, 0)),
                pl.BlockSpec((1, imps, width), lambda i, at_ref: (i // 2, 0, 0)),
                pl.BlockSpec((1, imps, width), lambda i, at_ref: (i // 2, 0, 0)),
            ],
            out_specs=[
                pl.BlockSpec((rows, width), fixed),
                pl.BlockSpec((rows, PANEL), fixed),
                pl.BlockSpec((1, width), fixed),
            ],
            scratch_shapes=[
                pltpu.VMEM((width, rows + PANEL), f32),
                pltpu.VMEM((PANEL, rows), f32),
                pltpu.VMEM((PANEL, PANEL), f32),
                pltpu.VMEM((feat, width), f32),
                pltpu.VMEM((PANEL, PANEL), f32),
                pltpu.VMEM((PANEL, 2 * PANEL), f32),
                pltpu.VMEM((128, 256), f32),
            ],
        ),
        compiler_params=pltpu.CompilerParams(vmem_limit_bytes=50 << 20),
        name="gram_schur",
    )(at, gathered, near, far)


def per_device(embeddings, frequencies, phases, treat_freq, treatment, flips, panel):
    imps = embeddings.shape[0]
    width = frequencies.shape[1]
    samp = lax.axis_size(SAMP)
    feat = lax.axis_size(FEAT)
    samp_index = lax.axis_index(SAMP)
    feat_index = lax.axis_index(FEAT)
    count = imps * samp
    rows = width * feat // samp
    piece = imps // feat
    elim = PANEL // width

    project = jnp.dot(embeddings, frequencies, preferred_element_type=f32)
    treated = treatment.astype(f32)
    flipped = flips.astype(f32)
    counter = treated + flipped - 2.0 * treated * flipped
    base = project + phases[None, :]
    observed = cosine(base + treated[:, None] * treat_freq[None, :])
    counterfactual = cosine(base + counter[:, None] * treat_freq[None, :])
    moment_part = jnp.sum(counterfactual - observed, axis=0)
    feature = observed.astype(bf16)

    near = lax.all_gather(feature, "x")
    swapped = lax.ppermute(feature, "zh", [(0, 1), (1, 0)])

    shares = lax.all_to_all(
        feature.reshape(feat, piece, width), FEAT, split_axis=0, concat_axis=0, tiled=True
    )
    swapped, shares = lax.optimization_barrier((swapped, shares))
    far = lax.all_gather(swapped, "x")
    first_dev = panel[0] * elim
    picked = lax.dynamic_slice_in_dim(shares, first_dev, elim, 0)
    high = lax.reduce_precision(moment_part, 8, 7)
    middle = lax.reduce_precision(moment_part - high, 8, 7)
    low = moment_part - high - middle
    moment_rows = jnp.pad(jnp.stack([high, middle, low]), ((0, 13), (0, 0))).astype(bf16)
    held = jnp.concatenate([picked.reshape(elim * piece, width), moment_rows], axis=0)
    send = jnp.concatenate(
        [
            shares.reshape(samp, feat // samp * piece, width),
            jnp.broadcast_to(held[None], (samp,) + held.shape),
        ],
        axis=1,
    )
    share = lax.all_to_all(send, SAMP, split_axis=0, concat_axis=0, tiled=True)
    gathered = lax.all_gather(share, FEAT)

    at = jnp.stack(
        [
            samp_index * rows,
            feat_index * width,
            panel[0] * PANEL,
            lax.axis_index("zh"),
            feat_index,
            first_dev,
        ]
    ).astype(jnp.int32)
    schur, factor, reduced = gram_schur(count, at, gathered, near, far)
    return (schur, factor, reduced[0])


def solution(mesh):
    fine = Mesh(mesh.devices.reshape(4, 2, 4, 4, 2), ("x", "zh", "y", "zl", "core"))
    return jax.shard_map(
        per_device,
        mesh=fine,
        in_specs=(P(SAMP, None), P(None, FEAT), P(FEAT), P(FEAT), P(SAMP), P(SAMP), P()),
        out_specs=(P(SAMP, FEAT), P(SAMP, None), P(FEAT)),
        check_vma=False,
    )
```

```python
import jax
import jax.numpy as jnp
from jax import lax
from jax.experimental import pallas as pl
from jax.experimental.pallas import tpu as pltpu
from jax.sharding import Mesh
from jax.sharding import PartitionSpec as P

PANEL = 512
ridge = 0.1
f32 = jnp.float32
bf16 = jnp.bfloat16
HIGHEST = lax.Precision.HIGHEST

SAMP = ("x", "zh")
FEAT = ("y", "zl", "core")

SINE = (
    -8.885765875337938,
    58.46599556065702,
    -115.4071939365197,
    108.47536728137668,
    -59.39695452559278,
    20.275610646954046,
)


def cosine(x):
    turns = x * 0.15915494309189535
    s = jnp.abs(turns - jnp.round(turns)) - 0.25
    u = s * s
    p = SINE[5]
    for c in SINE[4::-1]:
        p = p * u + c
    return s * p


def dot(left, right, dims, **kw):
    return lax.dot_general(left, right, (dims, ((), ())), preferred_element_type=f32, **kw)


def invert_body(a_ref, out_ref, work, diag):
    n = a_ref.shape[0]
    nb = 128
    work[:, :n] = a_ref[...]
    row = lax.broadcasted_iota(jnp.int32, (n, n), 0)
    col = lax.broadcasted_iota(jnp.int32, (n, n), 1)
    work[:, n:] = (row == col).astype(f32)
    sub = lax.broadcasted_iota(jnp.int32, (8, nb), 0)
    lane = lax.broadcasted_iota(jnp.int32, (8, nb), 1)
    eye = (
        lax.broadcasted_iota(jnp.int32, (nb, nb), 0) == lax.broadcasted_iota(jnp.int32, (nb, nb), 1)
    ).astype(f32)
    for lo in range(0, n, nb):
        hi = lo + nb
        diag[:, :nb] = work[lo:hi, lo:hi]
        diag[:, nb:] = eye
        for q in range(0, nb, 8):
            ra = diag[q : q + 8, :nb]
            rb = diag[q : q + 8, nb:]
            cols = [jnp.broadcast_to(ra[:, q + c : q + c + 1], (8, nb)) for c in range(8)]
            pivots = jnp.ones((8, nb), f32)
            for c in range(8):
                d = jnp.broadcast_to(cols[c][c : c + 1, :], (8, nb))
                pivots = jnp.where(sub == c, d, pivots)
                if c < 7:
                    mult = jnp.where(sub > c, cols[c] / d, 0.0)
                    for e in range(c + 1, 8):
                        cols[e] = cols[e] - mult * jnp.broadcast_to(cols[e][c : c + 1, :], (8, nb))
                    ra = ra - mult * jnp.broadcast_to(ra[c : c + 1, :], (8, nb))
                    rb = rb - mult * jnp.broadcast_to(rb[c : c + 1, :], (8, nb))
            scale = lax.rsqrt(pivots)
            ra = ra * scale
            rb = rb * scale
            diag[q : q + 8, nb:] = rb
            if q + 8 < nb:
                low = jnp.where(lane >= q + 8, ra, 0.0)
                update = dot(low, jnp.concatenate([low, rb], 1), ((0,), (0,)), precision=HIGHEST)
                diag[q + 8 :, :] = diag[q + 8 :, :] - update[q + 8 :, :]
        upper = dot(diag[:, nb:], work[lo:hi, hi : n + hi], ((1,), (0,)), precision=HIGHEST)
        rest = n - hi
        out_ref[lo:hi, :hi] = upper[:, rest:]
        if rest:
            work[hi:, hi : n + hi] = work[hi:, hi : n + hi] - dot(
                upper[:, :rest], upper, ((0,), (0,)), precision=HIGHEST
            )
            out_ref[lo:hi, hi:] = jnp.zeros((nb, rest), f32)


def inverse_factor(pivot):
    n = pivot.shape[0]
    return pl.pallas_call(
        invert_body,
        out_shape=jax.ShapeDtypeStruct((n, n), f32),
        scratch_shapes=[pltpu.VMEM((n, 2 * n), f32), pltpu.VMEM((128, 256), f32)],
        compiler_params=pltpu.CompilerParams(vmem_limit_bytes=16 << 20),
        cost_estimate=pl.CostEstimate(flops=30 * 10**9, bytes_accessed=2 << 20, transcendentals=0),
        name="inverse_factor",
    )(pivot)


def split(a):
    high = a.astype(bf16)
    return high, (a - high.astype(f32)).astype(bf16)


def dot3(left, right, dims):
    lh, ll = left
    rh, rl = right
    return dot(lh, rh, dims) + (dot(lh, rl, dims) + dot(ll, rh, dims))


NN = ((1,), (0,))
NT = ((1,), (1,))


def gram_body(at_ref, all_ref, near_ref, own, panel, pivot):
    step = pl.program_id(0)
    imps = near_ref.shape[1]
    width = near_ref.shape[2]
    piece = imps // all_ref.shape[0]
    rows = panel.shape[1]
    row_blocks = rows // width
    blocks = row_blocks + PANEL // width

    @pl.when(step == 0)
    def _():
        own[...] = jnp.zeros_like(own)
        panel[...] = jnp.zeros_like(panel)
        pivot[...] = jnp.zeros_like(pivot)

    def block(b):
        return all_ref[:, 0, b * piece : (b + 1) * piece, :].reshape(imps, width)

    elim = jnp.concatenate([block(b) for b in range(row_blocks, blocks)], axis=1)
    elim_t = elim.T
    for b in range(row_blocks):
        at = slice(b * width, (b + 1) * width)
        panel[:, at] += dot(elim_t, block(b), NN)
    pivot[...] += dot(elim_t, elim, NN)

    @pl.when(step % 2 == at_ref[3])
    def _():
        mine_t = near_ref[0].T
        for b in range(blocks):
            at = slice(b * width, (b + 1) * width)
            own[:, at] += dot(mine_t, block(b), NN)


def gram_sums(at, gathered, near):
    feat, samp, held, width = gathered.shape
    imps = near.shape[1]
    rows = width * feat // samp
    fixed = lambda i, at_ref: (0, 0)
    shapes = [(width, rows + PANEL), (PANEL, rows), (PANEL, PANEL)]
    return pl.pallas_call(
        gram_body,
        out_shape=[jax.ShapeDtypeStruct(s, f32) for s in shapes],
        grid_spec=pltpu.PrefetchScalarGridSpec(
            num_scalar_prefetch=1,
            grid=(samp,),
            in_specs=[
                pl.BlockSpec((feat, 1, held, width), lambda i, at_ref: (0, i, 0, 0)),
                pl.BlockSpec((1, imps, width), lambda i, at_ref: (i // 2, 0, 0)),
            ],
            out_specs=[pl.BlockSpec(s, fixed) for s in shapes],
        ),
        compiler_params=pltpu.CompilerParams(vmem_limit_bytes=32 << 20),
        cost_estimate=pl.CostEstimate(flops=20 * 10**9, bytes_accessed=30 << 20, transcendentals=0),
        name="gram_sums",
    )(at, gathered, near)


def finish_body(
    count, at_ref, all_ref, far0, far1, far2, far3, near_sum, panel, inv_ref, m_ref, mk_ref,
    schur_ref, factor_ref, red_ref, far_sum, mine_ref,
):
    step = pl.program_id(0)
    imps, width = far0.shape
    piece = imps // all_ref.shape[0]
    rows = panel.shape[1]
    blocks = (rows + PANEL) // width
    for k, ref in enumerate((far0, far1, far2, far3)):

        @pl.when(((step - at_ref[4]) & 3) == k)
        def _():
            mine_ref[...] = ref[...].T

    mine_t = mine_ref[...]
    for b in range(blocks):
        at = slice(b * width, (b + 1) * width)
        part = dot(
            mine_t, all_ref[:, 0, b * piece : (b + 1) * piece, :].reshape(imps, width), NN
        )
        far_sum[:, at] = jnp.where(step == 0, part, far_sum[:, at] + part)

    @pl.when(step == pl.num_programs(0) - 1)
    def _():
        row0, col0, first = at_ref[0], at_ref[1], at_ref[2]
        scale = 1.0 / count

        def diagonal(shape, r0, c0):
            r = r0 + lax.broadcasted_iota(jnp.int32, shape, 0)
            c = c0 + lax.broadcasted_iota(jnp.int32, shape, 1)
            return jnp.where(r == c, ridge, 0.0)

        own = (near_sum[...] + far_sum[...]) * scale
        inv = split(inv_ref[...])
        cross = own[:, rows:] + diagonal((width, PANEL), col0, first)
        cross = dot3(split(cross), inv, NT)
        cross_parts = split(cross)
        for lo in range(0, rows, width):
            at = slice(lo, lo + width)
            cols = panel[:, at].T * scale + diagonal((width, PANEL), row0 + lo, first)
            factor = dot3(split(cols), inv, NT)
            factor_ref[at, :] = factor
            gram = own[:, at].T + diagonal((width, width), row0 + lo, col0)
            schur_ref[at, :] = gram - dot3(split(factor), cross_parts, NT)
        elim = jnp.broadcast_to(mk_ref[...], (8, PANEL))
        solved = dot(elim, inv_ref[...], NT, precision=HIGHEST)
        part = dot(solved, cross, NT, precision=HIGHEST)
        red_ref[...] = (m_ref[...] - part[:1]) * (count**0.5)


def finish(count, at, gathered, far, near_sum, panel, inv, m, mk):
    feat, samp, held, width = gathered.shape
    imps = far[0].shape[0]
    rows = width * feat // samp
    fixed = lambda i, at_ref: (0, 0)
    outs = [(rows, width), (rows, PANEL), (1, width)]
    whole = list(far) + [near_sum, panel, inv, m, mk]
    return pl.pallas_call(
        lambda *refs: finish_body(count, *refs),
        out_shape=[jax.ShapeDtypeStruct(s, f32) for s in outs],
        grid_spec=pltpu.PrefetchScalarGridSpec(
            num_scalar_prefetch=1,
            grid=(len(far),),
            in_specs=[
                pl.BlockSpec(
                    (feat, 1, held, width), lambda i, at_ref: (0, 2 * i + 1 - at_ref[3], 0, 0)
                )
            ]
            + [pl.BlockSpec(a.shape, fixed) for a in whole],
            out_specs=[pl.BlockSpec(s, fixed) for s in outs],
            scratch_shapes=[
                pltpu.VMEM((width, rows + PANEL), f32),
                pltpu.VMEM((width, imps), bf16),
            ],
        ),
        compiler_params=pltpu.CompilerParams(vmem_limit_bytes=44 << 20),
        cost_estimate=pl.CostEstimate(flops=9 * 10**9, bytes_accessed=24 << 20, transcendentals=0),
        name="finish",
    )(at, gathered, *whole)


def per_device(embeddings, frequencies, phases, treat_freq, treatment, flips, panel):
    imps = embeddings.shape[0]
    width = frequencies.shape[1]
    samp = lax.axis_size(SAMP)
    feat = lax.axis_size(FEAT)
    samp_index = lax.axis_index(SAMP)
    feat_index = lax.axis_index(FEAT)
    count = imps * samp
    rows = width * feat // samp
    piece = imps // feat
    elim = PANEL // width

    project = jnp.dot(embeddings, frequencies, preferred_element_type=f32)
    treated = treatment.astype(f32)
    flipped = flips.astype(f32)
    counter = treated + flipped - 2.0 * treated * flipped
    base = project + phases[None, :]
    observed = cosine(base + treated[:, None] * treat_freq[None, :])
    counterfactual = cosine(base + counter[:, None] * treat_freq[None, :])
    moment_part = jnp.sum(counterfactual - observed, axis=0)
    feature = observed.astype(bf16)

    near = lax.all_gather(feature, "x")

    shares = lax.all_to_all(
        feature.reshape(feat, piece, width), FEAT, split_axis=0, concat_axis=0, tiled=True
    )
    first_dev = panel[0] * elim
    picked = lax.dynamic_slice_in_dim(shares, first_dev, elim, 0).reshape(1, elim * piece, width)
    send = jnp.concatenate(
        [
            shares.reshape(samp, feat // samp * piece, width),
            jnp.broadcast_to(picked, (samp, elim * piece, width)),
        ],
        axis=1,
    )
    share = lax.all_to_all(send, SAMP, split_axis=0, concat_axis=0, tiled=True)
    share, near = lax.optimization_barrier((share, near))
    gathered = lax.all_gather(share, FEAT)

    share, moment_part = lax.optimization_barrier((share, moment_part))
    moment = lax.psum(moment_part, SAMP) / count
    moments = lax.all_gather(lax.all_gather(moment, ("zl", "core")), "y").reshape(-1)
    moment_panel = lax.dynamic_slice_in_dim(moments, panel[0] * PANEL, PANEL, 0)

    gathered, feature = lax.optimization_barrier((gathered, feature))
    swapped = lax.ppermute(feature, "zh", [(0, 1), (1, 0)])
    at = jnp.stack(
        [
            samp_index * rows,
            feat_index * width,
            panel[0] * PANEL,
            lax.axis_index("zh"),
            lax.axis_index("x"),
        ]
    ).astype(jnp.int32)
    near_sum, panel_sum, pivot_sum = gram_sums(at, gathered, near)
    swapped, pivot_sum = lax.optimization_barrier((swapped, pivot_sum))
    xs = lax.axis_size("x")
    far = [swapped] + [
        lax.ppermute(swapped, "x", [(i, (i - r) % xs) for i in range(xs)]) for r in range(1, xs)
    ]
    inv = inverse_factor(pivot_sum / count + ridge * jnp.eye(PANEL, dtype=f32))
    schur, factor, reduced = finish(
        count, at, gathered, far, near_sum, panel_sum, inv, moment[None], moment_panel[None]
    )
    return (schur, factor, reduced[0])


def solution(mesh):
    fine = Mesh(mesh.devices.reshape(4, 2, 4, 4, 2), ("x", "zh", "y", "zl", "core"))
    return jax.shard_map(
        per_device,
        mesh=fine,
        in_specs=(P(SAMP, None), P(None, FEAT), P(FEAT), P(FEAT), P(SAMP), P(SAMP), P()),
        out_specs=(P(SAMP, FEAT), P(SAMP, None), P(FEAT)),
        check_vma=False,
    )
```

```python
import jax
import jax.numpy as jnp
from jax import lax
from jax.experimental import pallas as pl
from jax.experimental.pallas import tpu as pltpu
from jax.sharding import Mesh
from jax.sharding import PartitionSpec as P

PANEL = 512
ridge = 0.1
f32 = jnp.float32
bf16 = jnp.bfloat16
HIGHEST = lax.Precision.HIGHEST

SAMP = ("x", "zh")
FEAT = ("y", "zl", "core")

SINE = (
    -8.885765875337938,
    58.46599556065702,
    -115.4071939365197,
    108.47536728137668,
    -59.39695452559278,
    20.275610646954046,
)


def cosine(x):
    turns = x * 0.15915494309189535
    s = jnp.abs(turns - jnp.round(turns)) - 0.25
    u = s * s
    p = SINE[5]
    for c in SINE[4::-1]:
        p = p * u + c
    return s * p


def dot(left, right, dims, **kw):
    return lax.dot_general(left, right, (dims, ((), ())), preferred_element_type=f32, **kw)


def split(a):
    high = a.astype(bf16)
    return high, (a - high.astype(f32)).astype(bf16)


def dot3(left, right, dims):
    lh, ll = left
    rh, rl = right
    return dot(lh, rh, dims) + (dot(lh, rl, dims) + dot(ll, rh, dims))


NN = ((1,), (0,))
NT = ((1,), (1,))


def eliminate(a_ref, out_ref, work, diag):
    n = a_ref.shape[0]
    nb = 128
    work[:, :n] = a_ref[...]
    row = lax.broadcasted_iota(jnp.int32, (n, n), 0)
    col = lax.broadcasted_iota(jnp.int32, (n, n), 1)
    work[:, n:] = (row == col).astype(f32)
    sub = lax.broadcasted_iota(jnp.int32, (8, nb), 0)
    lane = lax.broadcasted_iota(jnp.int32, (8, nb), 1)
    eye = (
        lax.broadcasted_iota(jnp.int32, (nb, nb), 0) == lax.broadcasted_iota(jnp.int32, (nb, nb), 1)
    ).astype(f32)
    for lo in range(0, n, nb):
        hi = lo + nb
        diag[:, :nb] = work[lo:hi, lo:hi]
        diag[:, nb:] = eye

        def slab(k, carry):
            q = pl.multiple_of(8 * k, 8)
            ra = diag[pl.ds(q, 8), :nb]
            rb = diag[pl.ds(q, 8), nb:]
            cols = [
                jnp.broadcast_to(
                    jnp.sum(jnp.where(lane == q + c, ra, 0.0), axis=1, keepdims=True), (8, nb)
                )
                for c in range(8)
            ]
            pivots = jnp.ones((8, nb), f32)
            for c in range(8):
                d = jnp.broadcast_to(cols[c][c : c + 1, :], (8, nb))
                pivots = jnp.where(sub == c, d, pivots)
                mult = jnp.where(sub > c, cols[c] / d, 0.0)
                for e in range(c + 1, 8):
                    cols[e] = cols[e] - mult * jnp.broadcast_to(cols[e][c : c + 1, :], (8, nb))
                ra = ra - mult * jnp.broadcast_to(ra[c : c + 1, :], (8, nb))
                rb = rb - mult * jnp.broadcast_to(rb[c : c + 1, :], (8, nb))
            scale = lax.rsqrt(pivots)
            ra = ra * scale
            rb = rb * scale
            diag[pl.ds(q, 8), nb:] = rb
            low = jnp.where(lane >= q + 8, ra, 0.0)
            update = dot(low, jnp.concatenate([low, rb], 1), ((0,), (0,)), precision=HIGHEST)
            diag[...] = diag[...] - update
            return carry

        lax.fori_loop(0, nb // 8, slab, 0)
        upper = dot(diag[:, nb:], work[lo:hi, hi : n + hi], ((1,), (0,)), precision=HIGHEST)
        rest = n - hi
        out_ref[lo:hi, :hi] = upper[:, rest:]
        if rest:
            work[hi:, hi : n + hi] = work[hi:, hi : n + hi] - dot(
                upper[:, :rest], upper, ((0,), (0,)), precision=HIGHEST
            )
            out_ref[lo:hi, hi:] = jnp.zeros((nb, rest), f32)


def inverse_body(a_ref, out_ref, work, diag, s_ref, t_ref):
    n = a_ref.shape[0]
    row = lax.broadcasted_iota(jnp.int32, (n, n), 0)
    col = lax.broadcasted_iota(jnp.int32, (n, n), 1)
    eye = row == col
    a = a_ref[...]
    picked = jnp.where(eye, a, 0.0)
    scale = lax.rsqrt(jnp.sum(picked, axis=0, keepdims=True))
    s_ref[...] = a * scale * lax.rsqrt(jnp.sum(picked, axis=1, keepdims=True))

    def lower(e):
        return jnp.where(row > col, e, jnp.where(eye, 0.5 * e, 0.0))

    one = eye.astype(f32)
    t_ref[...] = one - lower(s_ref[...] - one)
    s_high = s_ref[...].astype(bf16)
    for _ in range(2):
        t = t_ref[...].astype(bf16)
        e = dot(dot(t, s_high, NN).astype(bf16), t, NT) - one
        t_ref[...] = t_ref[...] - dot(lower(e).astype(bf16), t, NN)

    def unsettled(state):
        step, error = state
        return jnp.logical_and(step < 8, jnp.logical_not(error <= 1.6e-5))

    def refine(state):
        t = split(t_ref[...])
        e = dot3(split(dot3(t, split(s_ref[...]), NN)), t, NT) - one
        t_ref[...] = t_ref[...] - dot3(split(lower(e)), t, NN)
        return state[0] + 1, jnp.sum(e * e)

    _, error = lax.while_loop(unsettled, refine, (jnp.int32(0), jnp.float32(1.0)))
    t = t_ref[...]
    smallest = jnp.min(jnp.where(eye, t, 1.0))
    good = jnp.logical_and(error <= 1.6e-5, smallest > 0.0)

    @pl.when(good)
    def _():
        out_ref[...] = t_ref[...] * scale

    @pl.when(jnp.logical_not(good))
    def _():
        eliminate(a_ref, out_ref, work, diag)


def inverse_factor(pivot):
    n = pivot.shape[0]
    return pl.pallas_call(
        inverse_body,
        out_shape=jax.ShapeDtypeStruct((n, n), f32),
        scratch_shapes=[
            pltpu.VMEM((n, 2 * n), f32),
            pltpu.VMEM((128, 256), f32),
            pltpu.VMEM((n, n), f32),
            pltpu.VMEM((n, n), f32),
        ],
        compiler_params=pltpu.CompilerParams(vmem_limit_bytes=32 << 20),
        cost_estimate=pl.CostEstimate(flops=30 * 10**9, bytes_accessed=2 << 20, transcendentals=0),
        name="inverse_factor",
    )(pivot)


def gram_body(at_ref, all_ref, near_ref, own, panel, pivot):
    step = pl.program_id(0)
    imps = near_ref.shape[1]
    width = near_ref.shape[2]
    piece = imps // all_ref.shape[0]
    rows = panel.shape[1]
    row_blocks = rows // width
    blocks = row_blocks + PANEL // width

    @pl.when(step == 0)
    def _():
        own[...] = jnp.zeros_like(own)
        panel[...] = jnp.zeros_like(panel)
        pivot[...] = jnp.zeros_like(pivot)

    def block(b):
        return all_ref[:, 0, b * piece : (b + 1) * piece, :].reshape(imps, width)

    elim = jnp.concatenate([block(b) for b in range(row_blocks, blocks)], axis=1)
    elim_t = elim.T
    for b in range(row_blocks):
        at = slice(b * width, (b + 1) * width)
        panel[:, at] += dot(elim_t, block(b), NN)
    pivot[...] += dot(elim_t, elim, NN)

    @pl.when(step % 2 == at_ref[3])
    def _():
        mine_t = near_ref[0].T
        for b in range(blocks):
            at = slice(b * width, (b + 1) * width)
            own[:, at] += dot(mine_t, block(b), NN)


def gram_sums(at, gathered, near):
    feat, samp, held, width = gathered.shape
    imps = near.shape[1]
    rows = width * feat // samp
    fixed = lambda i, at_ref: (0, 0)
    shapes = [(width, rows + PANEL), (PANEL, rows), (PANEL, PANEL)]
    return pl.pallas_call(
        gram_body,
        out_shape=[jax.ShapeDtypeStruct(s, f32) for s in shapes],
        grid_spec=pltpu.PrefetchScalarGridSpec(
            num_scalar_prefetch=1,
            grid=(samp,),
            in_specs=[
                pl.BlockSpec((feat, 1, held, width), lambda i, at_ref: (0, i, 0, 0)),
                pl.BlockSpec((1, imps, width), lambda i, at_ref: (i // 2, 0, 0)),
            ],
            out_specs=[pl.BlockSpec(s, fixed) for s in shapes],
        ),
        compiler_params=pltpu.CompilerParams(vmem_limit_bytes=32 << 20),
        cost_estimate=pl.CostEstimate(flops=20 * 10**9, bytes_accessed=30 << 20, transcendentals=0),
        name="gram_sums",
    )(at, gathered, near)


def finish_body(
    count, at_ref, all_ref, far0, far1, far2, far3, near_sum, panel, inv_ref, m_ref, mk_ref,
    schur_ref, factor_ref, red_ref, far_sum, mine_ref,
):
    step = pl.program_id(0)
    imps, width = far0.shape
    piece = imps // all_ref.shape[0]
    rows = panel.shape[1]
    blocks = (rows + PANEL) // width
    for k, ref in enumerate((far0, far1, far2, far3)):

        @pl.when(((step - at_ref[4]) & 3) == k)
        def _():
            mine_ref[...] = ref[...].T

    mine_t = mine_ref[...]
    for b in range(blocks):
        at = slice(b * width, (b + 1) * width)
        part = dot(
            mine_t, all_ref[:, 0, b * piece : (b + 1) * piece, :].reshape(imps, width), NN
        )
        far_sum[:, at] = jnp.where(step == 0, part, far_sum[:, at] + part)

    @pl.when(step == pl.num_programs(0) - 1)
    def _():
        row0, col0, first = at_ref[0], at_ref[1], at_ref[2]
        scale = 1.0 / count

        def diagonal(shape, r0, c0):
            r = r0 + lax.broadcasted_iota(jnp.int32, shape, 0)
            c = c0 + lax.broadcasted_iota(jnp.int32, shape, 1)
            return jnp.where(r == c, ridge, 0.0)

        own = (near_sum[...] + far_sum[...]) * scale
        inv = split(inv_ref[...])
        cross = own[:, rows:] + diagonal((width, PANEL), col0, first)
        cross = dot3(split(cross), inv, NT)
        cross_parts = split(cross)
        for lo in range(0, rows, width):
            at = slice(lo, lo + width)
            cols = panel[:, at].T * scale + diagonal((width, PANEL), row0 + lo, first)
            factor = dot3(split(cols), inv, NT)
            factor_ref[at, :] = factor
            gram = own[:, at].T + diagonal((width, width), row0 + lo, col0)
            schur_ref[at, :] = gram - dot3(split(factor), cross_parts, NT)
        elim = jnp.broadcast_to(mk_ref[...], (8, PANEL))
        solved = dot(elim, inv_ref[...], NT, precision=HIGHEST)
        part = dot(solved, cross, NT, precision=HIGHEST)
        red_ref[...] = (m_ref[...] - part[:1]) * (count**0.5)


def finish(count, at, gathered, far, near_sum, panel, inv, m, mk):
    feat, samp, held, width = gathered.shape
    imps = far[0].shape[0]
    rows = width * feat // samp
    fixed = lambda i, at_ref: (0, 0)
    outs = [(rows, width), (rows, PANEL), (1, width)]
    whole = list(far) + [near_sum, panel, inv, m, mk]
    return pl.pallas_call(
        lambda *refs: finish_body(count, *refs),
        out_shape=[jax.ShapeDtypeStruct(s, f32) for s in outs],
        grid_spec=pltpu.PrefetchScalarGridSpec(
            num_scalar_prefetch=1,
            grid=(len(far),),
            in_specs=[
                pl.BlockSpec(
                    (feat, 1, held, width), lambda i, at_ref: (0, 2 * i + 1 - at_ref[3], 0, 0)
                )
            ]
            + [pl.BlockSpec(a.shape, fixed) for a in whole],
            out_specs=[pl.BlockSpec(s, fixed) for s in outs],
            scratch_shapes=[
                pltpu.VMEM((width, rows + PANEL), f32),
                pltpu.VMEM((width, imps), bf16),
            ],
        ),
        compiler_params=pltpu.CompilerParams(vmem_limit_bytes=44 << 20),
        cost_estimate=pl.CostEstimate(flops=9 * 10**9, bytes_accessed=24 << 20, transcendentals=0),
        name="finish",
    )(at, gathered, *whole)


def per_device(embeddings, frequencies, phases, treat_freq, treatment, flips, panel):
    imps = embeddings.shape[0]
    width = frequencies.shape[1]
    samp = lax.axis_size(SAMP)
    feat = lax.axis_size(FEAT)
    samp_index = lax.axis_index(SAMP)
    feat_index = lax.axis_index(FEAT)
    count = imps * samp
    rows = width * feat // samp
    piece = imps // feat
    elim = PANEL // width

    project = jnp.dot(embeddings, frequencies, preferred_element_type=f32)
    treated = treatment.astype(f32)
    flipped = flips.astype(f32)
    counter = treated + flipped - 2.0 * treated * flipped
    base = project + phases[None, :]
    observed = cosine(base + treated[:, None] * treat_freq[None, :])
    counterfactual = cosine(base + counter[:, None] * treat_freq[None, :])
    moment_part = jnp.sum(counterfactual - observed, axis=0)
    feature = observed.astype(bf16)

    near = lax.all_gather(feature, "x")

    shares = lax.all_to_all(
        feature.reshape(feat, piece, width), FEAT, split_axis=0, concat_axis=0, tiled=True
    )
    first_dev = panel[0] * elim
    picked = lax.dynamic_slice_in_dim(shares, first_dev, elim, 0).reshape(1, elim * piece, width)
    send = jnp.concatenate(
        [
            shares.reshape(samp, feat // samp * piece, width),
            jnp.broadcast_to(picked, (samp, elim * piece, width)),
        ],
        axis=1,
    )
    share = lax.all_to_all(send, SAMP, split_axis=0, concat_axis=0, tiled=True)
    share, near = lax.optimization_barrier((share, near))
    gathered = lax.all_gather(share, FEAT)

    share, moment_part = lax.optimization_barrier((share, moment_part))
    moment = lax.psum(moment_part, SAMP) / count
    moments = lax.all_gather(lax.all_gather(moment, ("zl", "core")), "y").reshape(-1)
    moment_panel = lax.dynamic_slice_in_dim(moments, panel[0] * PANEL, PANEL, 0)

    gathered, feature = lax.optimization_barrier((gathered, feature))
    swapped = lax.ppermute(feature, "zh", [(0, 1), (1, 0)])
    at = jnp.stack(
        [
            samp_index * rows,
            feat_index * width,
            panel[0] * PANEL,
            lax.axis_index("zh"),
            lax.axis_index("x"),
        ]
    ).astype(jnp.int32)
    near_sum, panel_sum, pivot_sum = gram_sums(at, gathered, near)
    swapped, pivot_sum = lax.optimization_barrier((swapped, pivot_sum))
    xs = lax.axis_size("x")
    far = [swapped] + [
        lax.ppermute(swapped, "x", [(i, (i - r) % xs) for i in range(xs)]) for r in range(1, xs)
    ]
    inv = inverse_factor(pivot_sum / count + ridge * jnp.eye(PANEL, dtype=f32))
    schur, factor, reduced = finish(
        count, at, gathered, far, near_sum, panel_sum, inv, moment[None], moment_panel[None]
    )
    return (schur, factor, reduced[0])


def solution(mesh):
    fine = Mesh(mesh.devices.reshape(4, 2, 4, 4, 2), ("x", "zh", "y", "zl", "core"))
    return jax.shard_map(
        per_device,
        mesh=fine,
        in_specs=(P(SAMP, None), P(None, FEAT), P(FEAT), P(FEAT), P(SAMP), P(SAMP), P()),
        out_specs=(P(SAMP, FEAT), P(SAMP, None), P(FEAT)),
        check_vma=False,
    )
```

```python
import jax
import jax.numpy as jnp
from jax import lax
from jax.experimental import pallas as pl
from jax.experimental.pallas import tpu as pltpu
from jax.sharding import Mesh
from jax.sharding import PartitionSpec as P

PANEL = 512
ridge = 0.1
f32 = jnp.float32
bf16 = jnp.bfloat16
HIGHEST = lax.Precision.HIGHEST

SAMP = ("x", "zh")
FEAT = ("y", "zl", "core")

SINE = (
    -8.885765875337938,
    58.46599556065702,
    -115.4071939365197,
    108.47536728137668,
    -59.39695452559278,
    20.275610646954046,
)


def cosine(x):
    turns = x * 0.15915494309189535
    s = jnp.abs(turns - jnp.round(turns)) - 0.25
    u = s * s
    p = SINE[5]
    for c in SINE[4::-1]:
        p = p * u + c
    return s * p


def dot(left, right, dims, **kw):
    return lax.dot_general(left, right, (dims, ((), ())), preferred_element_type=f32, **kw)


def split(a):
    high = a.astype(bf16)
    return high, (a - high.astype(f32)).astype(bf16)


def dot3(left, right, dims):
    lh, ll = left
    rh, rl = right
    return dot(lh, rh, dims) + (dot(lh, rl, dims) + dot(ll, rh, dims))


NN = ((1,), (0,))
NT = ((1,), (1,))


def invert_body(a_ref, out_ref, work, diag):
    n = a_ref.shape[0]
    nb = 128
    work[:, :n] = a_ref[...]
    row = lax.broadcasted_iota(jnp.int32, (n, n), 0)
    col = lax.broadcasted_iota(jnp.int32, (n, n), 1)
    work[:, n:] = (row == col).astype(f32)
    sub = lax.broadcasted_iota(jnp.int32, (8, nb), 0)
    lane = lax.broadcasted_iota(jnp.int32, (8, nb), 1)
    eye = (
        lax.broadcasted_iota(jnp.int32, (nb, nb), 0) == lax.broadcasted_iota(jnp.int32, (nb, nb), 1)
    ).astype(f32)
    for lo in range(0, n, nb):
        hi = lo + nb
        diag[:, :nb] = work[lo:hi, lo:hi]
        diag[:, nb:] = eye

        def slab(k, carry):
            q = pl.multiple_of(8 * k, 8)
            ra = diag[pl.ds(q, 8), :nb]
            rb = diag[pl.ds(q, 8), nb:]
            cols = [
                jnp.broadcast_to(
                    jnp.sum(jnp.where(lane == q + c, ra, 0.0), axis=1, keepdims=True), (8, nb)
                )
                for c in range(8)
            ]
            pivots = jnp.ones((8, nb), f32)
            for c in range(8):
                d = jnp.broadcast_to(cols[c][c : c + 1, :], (8, nb))
                pivots = jnp.where(sub == c, d, pivots)
                mult = jnp.where(sub > c, cols[c] / d, 0.0)
                for e in range(c + 1, 8):
                    cols[e] = cols[e] - mult * jnp.broadcast_to(cols[e][c : c + 1, :], (8, nb))
                ra = ra - mult * jnp.broadcast_to(ra[c : c + 1, :], (8, nb))
                rb = rb - mult * jnp.broadcast_to(rb[c : c + 1, :], (8, nb))
            scale = lax.rsqrt(pivots)
            ra = ra * scale
            rb = rb * scale
            diag[pl.ds(q, 8), nb:] = rb
            low = jnp.where(lane >= q + 8, ra, 0.0)
            update = dot(low, jnp.concatenate([low, rb], 1), ((0,), (0,)), precision=HIGHEST)
            diag[...] = diag[...] - update
            return carry

        lax.fori_loop(0, nb // 8, slab, 0)
        upper = dot(diag[:, nb:], work[lo:hi, hi : n + hi], ((1,), (0,)), precision=HIGHEST)
        rest = n - hi
        out_ref[lo:hi, :hi] = upper[:, rest:]
        if rest:
            work[hi:, hi : n + hi] = work[hi:, hi : n + hi] - dot(
                upper[:, :rest], upper, ((0,), (0,)), precision=HIGHEST
            )
            out_ref[lo:hi, hi:] = jnp.zeros((nb, rest), f32)


def inverse_factor(pivot):
    n = pivot.shape[0]
    return pl.pallas_call(
        invert_body,
        out_shape=jax.ShapeDtypeStruct((n, n), f32),
        scratch_shapes=[pltpu.VMEM((n, 2 * n), f32), pltpu.VMEM((128, 256), f32)],
        compiler_params=pltpu.CompilerParams(vmem_limit_bytes=16 << 20),
        cost_estimate=pl.CostEstimate(flops=30 * 10**9, bytes_accessed=2 << 20, transcendentals=0),
        name="inverse_factor",
    )(pivot)


def gram_body(
    count, at_ref, all_ref, near_ref, far0, far1, far2, far3, inv_ref, mom,
    schur_ref, factor_ref, red_ref, own, panel, mine_ref,
):
    step = pl.program_id(0)
    imps = near_ref.shape[1]
    width = near_ref.shape[2]
    feat = all_ref.shape[0]
    piece = imps // feat
    rows = panel.shape[1]
    row_blocks = rows // width
    blocks = row_blocks + PANEL // width

    @pl.when(step == 0)
    def _():
        own[...] = jnp.zeros_like(own)
        panel[...] = jnp.zeros_like(panel)

    near_step = step % 2 == at_ref[3]

    @pl.when(near_step)
    def _():
        mine_ref[...] = near_ref[0].T

    for k, ref in enumerate((far0, far1, far2, far3)):

        @pl.when(jnp.logical_not(near_step) & (((step // 2 - at_ref[6]) & 3) == k))
        def _():
            mine_ref[...] = ref[...].T

    block = [
        all_ref[:, 0, b * piece : (b + 1) * piece, :].reshape(imps, width) for b in range(blocks)
    ]
    mine_t = mine_ref[...]
    elim_t = jnp.concatenate(block[row_blocks:], axis=1).T
    for b in range(blocks):
        at = slice(b * width, (b + 1) * width)
        own[:, at] += dot(mine_t, block[b], ((1,), (0,)))
        if b < row_blocks:
            panel[:, at] += dot(elim_t, block[b], ((1,), (0,)))

    @pl.when(step == pl.num_programs(0) - 1)
    def _():
        row0, col0, first = at_ref[0], at_ref[1], at_ref[2]
        scale = 1.0 / count

        def diagonal(shape, r0, c0):
            r = r0 + lax.broadcasted_iota(jnp.int32, shape, 0)
            c = c0 + lax.broadcasted_iota(jnp.int32, shape, 1)
            return jnp.where(r == c, ridge, 0.0)

        inv = split(inv_ref[...])
        cross = own[:, rows:] * scale + diagonal((width, PANEL), col0, first)
        cross = dot3(split(cross), inv, NT)
        cross_parts = split(cross)
        for lo in range(0, rows, width):
            at = slice(lo, lo + width)
            cols = panel[:, at].T * scale + diagonal((width, PANEL), row0 + lo, first)
            factor = dot3(split(cols), inv, NT)
            factor_ref[at, :] = factor
            gram = own[:, at].T * scale + diagonal((width, width), row0 + lo, col0)
            schur_ref[at, :] = gram - dot3(split(factor), cross_parts, NT)
        own_dev = at_ref[4]
        first_dev = at_ref[5]
        picked = [mom[pl.ds(first_dev + k, 1), :] for k in range(PANEL // width)]
        elim = jnp.broadcast_to(jnp.concatenate(picked, axis=1), (8, PANEL))
        solved = dot(elim, inv_ref[...], NT, precision=HIGHEST)
        part = dot(solved, cross, NT, precision=HIGHEST)
        reduced = mom[pl.ds(own_dev, 1), :] - part[:1]
        red_ref[...] = reduced * (count**0.5)


def gram_schur(count, at, gathered, near, far, inv, moments):
    feat, samp, held, width = gathered.shape
    imps = near.shape[1]
    rows = width * feat // samp
    fixed = lambda i, at_ref: (0, 0)
    whole = list(far) + [inv, moments]
    return pl.pallas_call(
        lambda *refs: gram_body(count, *refs),
        out_shape=(
            jax.ShapeDtypeStruct((rows, width), f32),
            jax.ShapeDtypeStruct((rows, PANEL), f32),
            jax.ShapeDtypeStruct((1, width), f32),
        ),
        grid_spec=pltpu.PrefetchScalarGridSpec(
            num_scalar_prefetch=1,
            grid=(samp,),
            in_specs=[
                pl.BlockSpec((feat, 1, held, width), lambda i, at_ref: (0, i, 0, 0)),
                pl.BlockSpec((1, imps, width), lambda i, at_ref: (i // 2, 0, 0)),
            ]
            + [pl.BlockSpec(a.shape, fixed) for a in whole],
            out_specs=[
                pl.BlockSpec((rows, width), fixed),
                pl.BlockSpec((rows, PANEL), fixed),
                pl.BlockSpec((1, width), fixed),
            ],
            scratch_shapes=[
                pltpu.VMEM((width, rows + PANEL), f32),
                pltpu.VMEM((PANEL, rows), f32),
                pltpu.VMEM((width, imps), bf16),
            ],
        ),
        compiler_params=pltpu.CompilerParams(vmem_limit_bytes=50 << 20),
        cost_estimate=pl.CostEstimate(flops=20 * 10**9, bytes_accessed=30 << 20, transcendentals=0),
        name="gram_schur",
    )(at, gathered, near, *whole)


def per_device(embeddings, frequencies, phases, treat_freq, treatment, flips, panel):
    imps = embeddings.shape[0]
    width = frequencies.shape[1]
    samp = lax.axis_size(SAMP)
    feat = lax.axis_size(FEAT)
    samp_index = lax.axis_index(SAMP)
    feat_index = lax.axis_index(FEAT)
    count = imps * samp
    rows = width * feat // samp
    piece = imps // feat
    elim = PANEL // width

    project = jnp.dot(embeddings, frequencies, preferred_element_type=f32)
    treated = treatment.astype(f32)
    flipped = flips.astype(f32)
    counter = treated + flipped - 2.0 * treated * flipped
    base = project + phases[None, :]
    observed = cosine(base + treated[:, None] * treat_freq[None, :])
    counterfactual = cosine(base + counter[:, None] * treat_freq[None, :])
    moment_part = jnp.sum(counterfactual - observed, axis=0)
    feature = observed.astype(bf16)

    near = lax.all_gather(feature, "x")

    shares = lax.all_to_all(
        feature.reshape(feat, piece, width), FEAT, split_axis=0, concat_axis=0, tiled=True
    )
    first_dev = panel[0] * elim
    picked = lax.dynamic_slice_in_dim(shares, first_dev, elim, 0).reshape(1, elim * piece, width)
    send = jnp.concatenate(
        [
            shares.reshape(samp, feat // samp * piece, width),
            jnp.broadcast_to(picked, (samp, elim * piece, width)),
        ],
        axis=1,
    )
    share = lax.all_to_all(send, SAMP, split_axis=0, concat_axis=0, tiled=True)
    share, near = lax.optimization_barrier((share, near))
    gathered = lax.all_gather(share, FEAT)

    share, feature, moment_part = lax.optimization_barrier((share, feature, moment_part))
    swapped = lax.ppermute(feature, "zh", [(0, 1), (1, 0)])
    skip = feat // samp * piece
    mine = jnp.concatenate(
        [
            share[:, skip + k * piece : skip + (k + 1) * piece, :].reshape(samp * piece, width)
            for k in range(elim)
        ],
        axis=1,
    )
    part_rows = PANEL // samp
    left = lax.dynamic_slice_in_dim(mine, samp_index * part_rows, part_rows, 1)
    partial = dot(left, mine, ((0,), (0,))).reshape(feat, part_rows // feat * PANEL)
    slabs = lax.all_to_all(partial, FEAT, split_axis=0, concat_axis=0, tiled=True)
    held = jnp.concatenate([jnp.sum(slabs, axis=0), moment_part])[None]
    held = lax.all_gather(held, ("zl", "core"), axis=0, tiled=True)
    held = lax.all_gather(held, "y", axis=0, tiled=True)
    other = lax.ppermute(held, "zh", [(0, 1), (1, 0)])
    lower = lax.axis_index("zh") == 0
    pair = jnp.stack([jnp.where(lower, held, other), jnp.where(lower, other, held)])
    xs = lax.axis_size("x")
    table = lax.all_to_all(
        jnp.broadcast_to(pair[None], (xs,) + pair.shape), "x", split_axis=0, concat_axis=0, tiled=True
    )
    far = [swapped] + [
        lax.ppermute(swapped, "x", [(i, (i - r) % xs) for i in range(xs)]) for r in range(1, xs)
    ]
    cut = part_rows // feat * PANEL
    pivot = table[..., :cut].reshape(PANEL, PANEL) / count
    moments = jnp.sum(table[..., cut:].reshape(samp, feat, width), axis=0) / count
    inv = inverse_factor(pivot + ridge * jnp.eye(PANEL, dtype=f32))

    at = jnp.stack(
        [
            samp_index * rows,
            feat_index * width,
            panel[0] * PANEL,
            lax.axis_index("zh"),
            feat_index,
            first_dev,
            lax.axis_index("x"),
        ]
    ).astype(jnp.int32)
    schur, factor, reduced = gram_schur(count, at, gathered, near, far, inv, moments)
    return (schur, factor, reduced[0])


def solution(mesh):
    fine = Mesh(mesh.devices.reshape(4, 2, 4, 4, 2), ("x", "zh", "y", "zl", "core"))
    return jax.shard_map(
        per_device,
        mesh=fine,
        in_specs=(P(SAMP, None), P(None, FEAT), P(FEAT), P(FEAT), P(SAMP), P(SAMP), P()),
        out_specs=(P(SAMP, FEAT), P(SAMP, None), P(FEAT)),
        check_vma=False,
    )
```

```python
import jax
import jax.numpy as jnp
from jax import lax
from jax.experimental import pallas as pl
from jax.experimental.pallas import tpu as pltpu
from jax.sharding import Mesh
from jax.sharding import PartitionSpec as P

PANEL = 512
ridge = 0.1
f32 = jnp.float32
bf16 = jnp.bfloat16
HIGHEST = lax.Precision.HIGHEST

SAMP = ("x", "zh")
FEAT = ("y", "zl", "core")
ZED = ("zh", "zl")

SINE = (
    -8.885765875337938,
    58.46599556065702,
    -115.4071939365197,
    108.47536728137668,
    -59.39695452559278,
    20.275610646954046,
)


def cosine(x):
    turns = x * 0.15915494309189535
    s = jnp.abs(turns - jnp.round(turns)) - 0.25
    u = s * s
    p = SINE[5]
    for c in SINE[4::-1]:
        p = p * u + c
    return s * p


def dot(left, right, dims, **kw):
    return lax.dot_general(left, right, (dims, ((), ())), preferred_element_type=f32, **kw)


def split(a):
    high = a.astype(bf16)
    return high, (a - high.astype(f32)).astype(bf16)


def dot3(left, right, dims):
    lh, ll = left
    rh, rl = right
    return dot(lh, rh, dims) + (dot(lh, rl, dims) + dot(ll, rh, dims))


NN = ((1,), (0,))
NT = ((1,), (1,))


def invert_body(a_ref, out_ref, work, diag):
    n = a_ref.shape[0]
    nb = 128
    work[:, :n] = a_ref[...]
    row = lax.broadcasted_iota(jnp.int32, (n, n), 0)
    col = lax.broadcasted_iota(jnp.int32, (n, n), 1)
    work[:, n:] = (row == col).astype(f32)
    sub = lax.broadcasted_iota(jnp.int32, (8, nb), 0)
    lane = lax.broadcasted_iota(jnp.int32, (8, nb), 1)
    eye = (
        lax.broadcasted_iota(jnp.int32, (nb, nb), 0) == lax.broadcasted_iota(jnp.int32, (nb, nb), 1)
    ).astype(f32)
    for lo in range(0, n, nb):
        hi = lo + nb
        diag[:, :nb] = work[lo:hi, lo:hi]
        diag[:, nb:] = eye

        def slab(k, carry):
            q = pl.multiple_of(8 * k, 8)
            ra = diag[pl.ds(q, 8), :nb]
            rb = diag[pl.ds(q, 8), nb:]
            cols = [
                jnp.broadcast_to(
                    jnp.sum(jnp.where(lane == q + c, ra, 0.0), axis=1, keepdims=True), (8, nb)
                )
                for c in range(8)
            ]
            pivots = jnp.ones((8, nb), f32)
            for c in range(8):
                d = jnp.broadcast_to(cols[c][c : c + 1, :], (8, nb))
                pivots = jnp.where(sub == c, d, pivots)
                mult = jnp.where(sub > c, cols[c] / d, 0.0)
                for e in range(c + 1, 8):
                    cols[e] = cols[e] - mult * jnp.broadcast_to(cols[e][c : c + 1, :], (8, nb))
                ra = ra - mult * jnp.broadcast_to(ra[c : c + 1, :], (8, nb))
                rb = rb - mult * jnp.broadcast_to(rb[c : c + 1, :], (8, nb))
            scale = lax.rsqrt(pivots)
            ra = ra * scale
            rb = rb * scale
            diag[pl.ds(q, 8), nb:] = rb
            low = jnp.where(lane >= q + 8, ra, 0.0)
            update = dot(low, jnp.concatenate([low, rb], 1), ((0,), (0,)), precision=HIGHEST)
            diag[...] = diag[...] - update
            return carry

        lax.fori_loop(0, nb // 8, slab, 0)
        upper = dot(diag[:, nb:], work[lo:hi, hi : n + hi], ((1,), (0,)), precision=HIGHEST)
        rest = n - hi
        out_ref[lo:hi, :hi] = upper[:, rest:]
        if rest:
            work[hi:, hi : n + hi] = work[hi:, hi : n + hi] - dot(
                upper[:, :rest], upper, ((0,), (0,)), precision=HIGHEST
            )
            out_ref[lo:hi, hi:] = jnp.zeros((nb, rest), f32)


def inverse_factor(pivot):
    n = pivot.shape[0]
    return pl.pallas_call(
        invert_body,
        out_shape=jax.ShapeDtypeStruct((n, n), f32),
        scratch_shapes=[pltpu.VMEM((n, 2 * n), f32), pltpu.VMEM((128, 256), f32)],
        compiler_params=pltpu.CompilerParams(vmem_limit_bytes=16 << 20),
        cost_estimate=pl.CostEstimate(flops=30 * 10**9, bytes_accessed=2 << 20, transcendentals=0),
        name="inverse_factor",
    )(pivot)


def gram_body(
    count, at_ref, all_ref, near_ref, far0, far1, far2, far3, inv_ref, mom,
    schur_ref, factor_ref, red_ref, own, panel, mine_ref,
):
    step = pl.program_id(0)
    imps = near_ref.shape[1]
    width = near_ref.shape[2]
    feat = all_ref.shape[0]
    piece = imps // feat
    rows = panel.shape[1]
    row_blocks = rows // width
    blocks = row_blocks + PANEL // width

    @pl.when(step == 0)
    def _():
        own[...] = jnp.zeros_like(own)
        panel[...] = jnp.zeros_like(panel)

    near_step = step % 2 == at_ref[3]

    @pl.when(near_step)
    def _():
        mine_ref[...] = near_ref[0].T

    for k, ref in enumerate((far0, far1, far2, far3)):

        @pl.when(jnp.logical_not(near_step) & (((step // 2 - at_ref[6]) & 3) == k))
        def _():
            mine_ref[...] = ref[...].T

    block = [
        all_ref[:, 0, b * piece : (b + 1) * piece, :].reshape(imps, width) for b in range(blocks)
    ]
    mine_t = mine_ref[...]
    elim_t = jnp.concatenate(block[row_blocks:], axis=1).T
    for b in range(blocks):
        at = slice(b * width, (b + 1) * width)
        own[:, at] += dot(mine_t, block[b], ((1,), (0,)))
        if b < row_blocks:
            panel[:, at] += dot(elim_t, block[b], ((1,), (0,)))

    @pl.when(step == pl.num_programs(0) - 1)
    def _():
        row0, col0, first = at_ref[0], at_ref[1], at_ref[2]
        scale = 1.0 / count

        def diagonal(shape, r0, c0):
            r = r0 + lax.broadcasted_iota(jnp.int32, shape, 0)
            c = c0 + lax.broadcasted_iota(jnp.int32, shape, 1)
            return jnp.where(r == c, ridge, 0.0)

        inv = split(inv_ref[...])
        cross = own[:, rows:] * scale + diagonal((width, PANEL), col0, first)
        cross = dot3(split(cross), inv, NT)
        cross_parts = split(cross)
        for lo in range(0, rows, width):
            at = slice(lo, lo + width)
            cols = panel[:, at].T * scale + diagonal((width, PANEL), row0 + lo, first)
            factor = dot3(split(cols), inv, NT)
            factor_ref[at, :] = factor
            gram = own[:, at].T * scale + diagonal((width, width), row0 + lo, col0)
            schur_ref[at, :] = gram - dot3(split(factor), cross_parts, NT)
        own_dev = at_ref[4]
        first_dev = at_ref[5]
        picked = [mom[pl.ds(first_dev + k, 1), :] for k in range(PANEL // width)]
        elim = jnp.broadcast_to(jnp.concatenate(picked, axis=1), (8, PANEL))
        solved = dot(elim, inv_ref[...], NT, precision=HIGHEST)
        part = dot(solved, cross, NT, precision=HIGHEST)
        reduced = mom[pl.ds(own_dev, 1), :] - part[:1]
        red_ref[...] = reduced * (count**0.5)


def gram_schur(count, at, gathered, near, far, inv, moments):
    feat, samp, held, width = gathered.shape
    imps = near.shape[1]
    rows = width * feat // samp
    fixed = lambda i, at_ref: (0, 0)
    whole = list(far) + [inv, moments]
    return pl.pallas_call(
        lambda *refs: gram_body(count, *refs),
        out_shape=(
            jax.ShapeDtypeStruct((rows, width), f32),
            jax.ShapeDtypeStruct((rows, PANEL), f32),
            jax.ShapeDtypeStruct((1, width), f32),
        ),
        grid_spec=pltpu.PrefetchScalarGridSpec(
            num_scalar_prefetch=1,
            grid=(samp,),
            in_specs=[
                pl.BlockSpec((feat, 1, held, width), lambda i, at_ref: (0, i, 0, 0)),
                pl.BlockSpec((1, imps, width), lambda i, at_ref: (i // 2, 0, 0)),
            ]
            + [pl.BlockSpec(a.shape, fixed) for a in whole],
            out_specs=[
                pl.BlockSpec((rows, width), fixed),
                pl.BlockSpec((rows, PANEL), fixed),
                pl.BlockSpec((1, width), fixed),
            ],
            scratch_shapes=[
                pltpu.VMEM((width, rows + PANEL), f32),
                pltpu.VMEM((PANEL, rows), f32),
                pltpu.VMEM((width, imps), bf16),
            ],
        ),
        compiler_params=pltpu.CompilerParams(vmem_limit_bytes=50 << 20),
        cost_estimate=pl.CostEstimate(flops=20 * 10**9, bytes_accessed=30 << 20, transcendentals=0),
        name="gram_schur",
    )(at, gathered, near, *whole)


def per_device(embeddings, frequencies, phases, treat_freq, treatment, flips, panel):
    imps = embeddings.shape[0]
    width = frequencies.shape[1]
    samp = lax.axis_size(SAMP)
    feat = lax.axis_size(FEAT)
    samp_index = lax.axis_index(SAMP)
    feat_index = lax.axis_index(FEAT)
    count = imps * samp
    rows = width * feat // samp
    piece = imps // feat
    elim = PANEL // width

    project = jnp.dot(embeddings, frequencies, preferred_element_type=f32)
    treated = treatment.astype(f32)
    flipped = flips.astype(f32)
    counter = treated + flipped - 2.0 * treated * flipped
    base = project + phases[None, :]
    observed = cosine(base + treated[:, None] * treat_freq[None, :])
    counterfactual = cosine(base + counter[:, None] * treat_freq[None, :])
    moment_part = jnp.sum(counterfactual - observed, axis=0)
    feature = observed.astype(bf16)

    near = lax.all_gather(feature, "x")

    shares = lax.all_to_all(
        feature.reshape(feat, piece, width), FEAT, split_axis=0, concat_axis=0, tiled=True
    )
    first_dev = panel[0] * elim
    picked = lax.dynamic_slice_in_dim(shares, first_dev, elim, 0).reshape(1, elim * piece, width)
    send = jnp.concatenate(
        [
            shares.reshape(samp, feat // samp * piece, width),
            jnp.broadcast_to(picked, (samp, elim * piece, width)),
        ],
        axis=1,
    )
    share = lax.all_to_all(send, SAMP, split_axis=0, concat_axis=0, tiled=True)
    share, near = lax.optimization_barrier((share, near))
    gathered = lax.all_gather(share, FEAT)

    share, feature, moment_part = lax.optimization_barrier((share, feature, moment_part))
    half = imps // 2
    zs = lax.axis_size(ZED)
    upward = [(i, (i + zs // 4) % zs) for i in range(zs)]
    downward = [(i, (i - zs // 4) % zs) for i in range(zs)]
    first = lax.ppermute(feature[:half], ZED, upward)
    second = lax.ppermute(feature[half:], ZED, downward)
    skip = feat // samp * piece
    mine = jnp.concatenate(
        [
            share[:, skip + k * piece : skip + (k + 1) * piece, :].reshape(samp * piece, width)
            for k in range(elim)
        ],
        axis=1,
    )
    part_rows = PANEL // samp
    left = lax.dynamic_slice_in_dim(mine, samp_index * part_rows, part_rows, 1)
    partial = dot(left, mine, ((0,), (0,))).reshape(feat, part_rows // feat * PANEL)
    slabs = lax.all_to_all(partial, FEAT, split_axis=0, concat_axis=0, tiled=True)
    held = jnp.concatenate([jnp.sum(slabs, axis=0), moment_part])[None]
    held, first, second = lax.optimization_barrier((held, first, second))
    first = lax.ppermute(first, ZED, upward)
    second = lax.ppermute(second, ZED, downward)
    held = lax.all_gather(held, ("zl", "core"), axis=0, tiled=True)
    held = lax.all_gather(held, "y", axis=0, tiled=True)
    held, first, second = lax.optimization_barrier((held, first, second))
    swapped = jnp.concatenate([first, second], axis=0)
    xs = lax.axis_size("x")
    far = [swapped] + [
        lax.ppermute(swapped, "x", [(i, (i - r) % xs) for i in range(xs)]) for r in range(1, xs)
    ]
    other = lax.ppermute(held, "zh", [(0, 1), (1, 0)])
    lower = lax.axis_index("zh") == 0
    pair = jnp.stack([jnp.where(lower, held, other), jnp.where(lower, other, held)])
    table = lax.all_to_all(
        jnp.broadcast_to(pair[None], (xs,) + pair.shape), "x", split_axis=0, concat_axis=0, tiled=True
    )
    cut = part_rows // feat * PANEL
    pivot = table[..., :cut].reshape(PANEL, PANEL) / count
    moments = jnp.sum(table[..., cut:].reshape(samp, feat, width), axis=0) / count
    inv = inverse_factor(pivot + ridge * jnp.eye(PANEL, dtype=f32))

    at = jnp.stack(
        [
            samp_index * rows,
            feat_index * width,
            panel[0] * PANEL,
            lax.axis_index("zh"),
            feat_index,
            first_dev,
            lax.axis_index("x"),
        ]
    ).astype(jnp.int32)
    schur, factor, reduced = gram_schur(count, at, gathered, near, far, inv, moments)
    return (schur, factor, reduced[0])


def solution(mesh):
    fine = Mesh(mesh.devices.reshape(4, 2, 4, 4, 2), ("x", "zh", "y", "zl", "core"))
    return jax.shard_map(
        per_device,
        mesh=fine,
        in_specs=(P(SAMP, None), P(None, FEAT), P(FEAT), P(FEAT), P(SAMP), P(SAMP), P()),
        out_specs=(P(SAMP, FEAT), P(SAMP, None), P(FEAT)),
        check_vma=False,
    )
```

```python
import jax
import jax.numpy as jnp
from jax import lax
from jax.experimental import pallas as pl
from jax.experimental.pallas import tpu as pltpu
from jax.sharding import Mesh
from jax.sharding import PartitionSpec as P

PANEL = 512
ridge = 0.1
f32 = jnp.float32
bf16 = jnp.bfloat16
HIGHEST = lax.Precision.HIGHEST

SAMP = ("x", "zh")
FEAT = ("y", "zl", "core")

SINE = (
    -8.885765875337938,
    58.46599556065702,
    -115.4071939365197,
    108.47536728137668,
    -59.39695452559278,
    20.275610646954046,
)


def cosine(x):
    turns = x * 0.15915494309189535
    s = jnp.abs(turns - jnp.round(turns)) - 0.25
    u = s * s
    p = SINE[5]
    for c in SINE[4::-1]:
        p = p * u + c
    return s * p


def dot(left, right, dims, **kw):
    return lax.dot_general(left, right, (dims, ((), ())), preferred_element_type=f32, **kw)


NN = ((1,), (0,))
NT = ((1,), (1,))


def invert_body(a_ref, out_ref, work, diag):
    n = a_ref.shape[0]
    nb = 128
    work[:, :n] = a_ref[...]
    row = lax.broadcasted_iota(jnp.int32, (n, n), 0)
    col = lax.broadcasted_iota(jnp.int32, (n, n), 1)
    work[:, n:] = (row == col).astype(f32)
    sub = lax.broadcasted_iota(jnp.int32, (8, nb), 0)
    lane = lax.broadcasted_iota(jnp.int32, (8, nb), 1)
    eye = (
        lax.broadcasted_iota(jnp.int32, (nb, nb), 0) == lax.broadcasted_iota(jnp.int32, (nb, nb), 1)
    ).astype(f32)
    for lo in range(0, n, nb):
        hi = lo + nb
        diag[:, :nb] = work[lo:hi, lo:hi]
        diag[:, nb:] = eye

        def slab(k, carry):
            q = pl.multiple_of(8 * k, 8)
            ra = diag[pl.ds(q, 8), :nb]
            rb = diag[pl.ds(q, 8), nb:]
            cols = [
                jnp.broadcast_to(
                    jnp.sum(jnp.where(lane == q + c, ra, 0.0), axis=1, keepdims=True), (8, nb)
                )
                for c in range(8)
            ]
            pivots = jnp.ones((8, nb), f32)
            for c in range(8):
                d = jnp.broadcast_to(cols[c][c : c + 1, :], (8, nb))
                pivots = jnp.where(sub == c, d, pivots)
                mult = jnp.where(sub > c, cols[c] / d, 0.0)
                for e in range(c + 1, 8):
                    cols[e] = cols[e] - mult * jnp.broadcast_to(cols[e][c : c + 1, :], (8, nb))
                ra = ra - mult * jnp.broadcast_to(ra[c : c + 1, :], (8, nb))
                rb = rb - mult * jnp.broadcast_to(rb[c : c + 1, :], (8, nb))
            scale = lax.rsqrt(pivots)
            ra = ra * scale
            rb = rb * scale
            diag[pl.ds(q, 8), nb:] = rb
            low = jnp.where(lane >= q + 8, ra, 0.0)
            update = dot(low, jnp.concatenate([low, rb], 1), ((0,), (0,)), precision=HIGHEST)
            diag[...] = diag[...] - update
            return carry

        lax.fori_loop(0, nb // 8, slab, 0)
        upper = dot(diag[:, nb:], work[lo:hi, hi : n + hi], ((1,), (0,)), precision=HIGHEST)
        rest = n - hi
        out_ref[lo:hi, :hi] = upper[:, rest:]
        if rest:
            work[hi:, hi : n + hi] = work[hi:, hi : n + hi] - dot(
                upper[:, :rest], upper, ((0,), (0,)), precision=HIGHEST
            )
            out_ref[lo:hi, hi:] = jnp.zeros((nb, rest), f32)


def inverse_factor(pivot):
    n = pivot.shape[0]
    return pl.pallas_call(
        invert_body,
        out_shape=jax.ShapeDtypeStruct((n, n), f32),
        scratch_shapes=[pltpu.VMEM((n, 2 * n), f32), pltpu.VMEM((128, 256), f32)],
        compiler_params=pltpu.CompilerParams(vmem_limit_bytes=16 << 20),
        cost_estimate=pl.CostEstimate(flops=30 * 10**9, bytes_accessed=2 << 20, transcendentals=0),
        name="inverse_factor",
    )(pivot)


def gram_body(
    count, at_ref, all_ref, near_ref, far0, far1, far2, far3, inv_ref, mom,
    schur_ref, factor_ref, red_ref, own, panel, mine_ref,
):
    step = pl.program_id(0)
    imps = near_ref.shape[1]
    width = near_ref.shape[2]
    feat = all_ref.shape[0]
    piece = imps // feat
    rows = panel.shape[1]
    row_blocks = rows // width
    blocks = row_blocks + PANEL // width

    @pl.when(step == 0)
    def _():
        own[...] = jnp.zeros_like(own)
        panel[...] = jnp.zeros_like(panel)

    zh = at_ref[3]
    mine_ref[zh] = near_ref[0].T
    for k, ref in enumerate((far0, far1, far2, far3)):

        @pl.when(((step - at_ref[6]) & 3) == k)
        def _():
            mine_ref[1 - zh] = ref[...].T

    def block(half, b):
        return all_ref[:, half, b * piece : (b + 1) * piece, :].reshape(imps, width)

    elim = [
        jnp.concatenate([block(half, b) for b in range(row_blocks, blocks)], axis=1)
        for half in range(2)
    ]
    left = [jnp.concatenate([mine_ref[half], elim[half].T], axis=0) for half in range(2)]
    both = jnp.concatenate(left, axis=1)
    for b in range(row_blocks):
        at = slice(b * width, (b + 1) * width)
        sums = dot(both, jnp.concatenate([block(0, b), block(1, b)], axis=0), NN)
        own[:, at] += sums[:width]
        panel[:, at] += sums[width:]
    own[:, rows:] += dot(mine_ref[0], elim[0], NN) + dot(mine_ref[1], elim[1], NN)

    @pl.when(step == pl.num_programs(0) - 1)
    def _():
        row0, col0, first = at_ref[0], at_ref[1], at_ref[2]
        scale = 1.0 / count

        def diagonal(shape, r0, c0):
            r = r0 + lax.broadcasted_iota(jnp.int32, shape, 0)
            c = c0 + lax.broadcasted_iota(jnp.int32, shape, 1)
            return jnp.where(r == c, ridge, 0.0)

        inv = inv_ref[...].T
        part = PANEL // 2

        def solve(a):
            return jnp.concatenate(
                [
                    dot(a[:, :part], inv[:part, :part], NN, precision=HIGHEST),
                    dot(a, inv[:, part:], NN, precision=HIGHEST),
                ],
                axis=1,
            )

        cross = own[:, rows:] * scale + diagonal((width, PANEL), col0, first)
        cross = solve(cross)
        cross_t = cross.T
        for lo in range(0, rows, width):
            at = slice(lo, lo + width)
            cols = panel[:, at].T * scale + diagonal((width, PANEL), row0 + lo, first)
            factor = solve(cols)
            factor_ref[at, :] = factor
            gram = own[:, at].T * scale + diagonal((width, width), row0 + lo, col0)
            schur_ref[at, :] = gram - dot(factor, cross_t, NN, precision=HIGHEST)
        own_dev = at_ref[4]
        first_dev = at_ref[5]
        picked = [mom[pl.ds(first_dev + k, 1), :] for k in range(PANEL // width)]
        elim = jnp.broadcast_to(jnp.concatenate(picked, axis=1), (8, PANEL))
        solved = dot(elim, inv_ref[...], NT, precision=HIGHEST)
        taken = dot(solved, cross, NT, precision=HIGHEST)
        reduced = mom[pl.ds(own_dev, 1), :] - taken[:1]
        red_ref[...] = reduced * (count**0.5)


def gram_schur(count, at, gathered, near, far, inv, moments):
    feat, samp, held, width = gathered.shape
    imps = near.shape[1]
    rows = width * feat // samp
    fixed = lambda i, at_ref: (0, 0)
    whole = list(far) + [inv, moments]
    return pl.pallas_call(
        lambda *refs: gram_body(count, *refs),
        out_shape=(
            jax.ShapeDtypeStruct((rows, width), f32),
            jax.ShapeDtypeStruct((rows, PANEL), f32),
            jax.ShapeDtypeStruct((1, width), f32),
        ),
        grid_spec=pltpu.PrefetchScalarGridSpec(
            num_scalar_prefetch=1,
            grid=(samp // 2,),
            in_specs=[
                pl.BlockSpec((feat, 2, held, width), lambda i, at_ref: (0, i, 0, 0)),
                pl.BlockSpec((1, imps, width), lambda i, at_ref: (i, 0, 0)),
            ]
            + [pl.BlockSpec(a.shape, fixed) for a in whole],
            out_specs=[
                pl.BlockSpec((rows, width), fixed),
                pl.BlockSpec((rows, PANEL), fixed),
                pl.BlockSpec((1, width), fixed),
            ],
            scratch_shapes=[
                pltpu.VMEM((width, rows + PANEL), f32),
                pltpu.VMEM((PANEL, rows), f32),
                pltpu.VMEM((2, width, imps), bf16),
            ],
        ),
        compiler_params=pltpu.CompilerParams(vmem_limit_bytes=50 << 20),
        cost_estimate=pl.CostEstimate(flops=20 * 10**9, bytes_accessed=30 << 20, transcendentals=0),
        name="gram_schur",
    )(at, gathered, near, *whole)


def per_device(embeddings, frequencies, phases, treat_freq, treatment, flips, panel):
    imps = embeddings.shape[0]
    width = frequencies.shape[1]
    samp = lax.axis_size(SAMP)
    feat = lax.axis_size(FEAT)
    samp_index = lax.axis_index(SAMP)
    feat_index = lax.axis_index(FEAT)
    count = imps * samp
    rows = width * feat // samp
    piece = imps // feat
    elim = PANEL // width

    project = jnp.dot(embeddings, frequencies, preferred_element_type=f32)
    treated = treatment.astype(f32)
    flipped = flips.astype(f32)
    counter = treated + flipped - 2.0 * treated * flipped
    base = project + phases[None, :]
    observed = cosine(base + treated[:, None] * treat_freq[None, :])
    counterfactual = cosine(base + counter[:, None] * treat_freq[None, :])
    moment_part = jnp.sum(counterfactual - observed, axis=0)
    feature = observed.astype(bf16)

    near = lax.all_gather(feature, "x")

    shares = lax.all_to_all(
        feature.reshape(feat, piece, width), FEAT, split_axis=0, concat_axis=0, tiled=True
    )
    first_dev = panel[0] * elim
    picked = lax.dynamic_slice_in_dim(shares, first_dev, elim, 0).reshape(1, elim * piece, width)
    send = jnp.concatenate(
        [
            shares.reshape(samp, feat // samp * piece, width),
            jnp.broadcast_to(picked, (samp, elim * piece, width)),
        ],
        axis=1,
    )
    share = lax.all_to_all(send, SAMP, split_axis=0, concat_axis=0, tiled=True)
    share, near = lax.optimization_barrier((share, near))
    gathered = lax.all_gather(share, FEAT)

    share, feature, moment_part = lax.optimization_barrier((share, feature, moment_part))
    swapped = lax.ppermute(feature, "zh", [(0, 1), (1, 0)])
    skip = feat // samp * piece
    mine = jnp.concatenate(
        [
            share[:, skip + k * piece : skip + (k + 1) * piece, :].reshape(samp * piece, width)
            for k in range(elim)
        ],
        axis=1,
    )
    part_rows = PANEL // samp
    left = lax.dynamic_slice_in_dim(mine, samp_index * part_rows, part_rows, 1)
    partial = dot(left, mine, ((0,), (0,))).reshape(feat, part_rows // feat * PANEL)
    slabs = lax.all_to_all(partial, FEAT, split_axis=0, concat_axis=0, tiled=True)
    held = jnp.concatenate([jnp.sum(slabs, axis=0), moment_part])[None]
    held = lax.all_gather(held, ("zl", "core"), axis=0, tiled=True)
    held = lax.all_gather(held, "y", axis=0, tiled=True)
    other = lax.ppermute(held, "zh", [(0, 1), (1, 0)])
    lower = lax.axis_index("zh") == 0
    pair = jnp.stack([jnp.where(lower, held, other), jnp.where(lower, other, held)])
    xs = lax.axis_size("x")
    table = lax.all_to_all(
        jnp.broadcast_to(pair[None], (xs,) + pair.shape), "x", split_axis=0, concat_axis=0, tiled=True
    )
    far = [swapped] + [
        lax.ppermute(swapped, "x", [(i, (i - r) % xs) for i in range(xs)]) for r in range(1, xs)
    ]
    cut = part_rows // feat * PANEL
    pivot = table[..., :cut].reshape(PANEL, PANEL) / count
    moments = jnp.sum(table[..., cut:].reshape(samp, feat, width), axis=0) / count
    inv = inverse_factor(pivot + ridge * jnp.eye(PANEL, dtype=f32))

    at = jnp.stack(
        [
            samp_index * rows,
            feat_index * width,
            panel[0] * PANEL,
            lax.axis_index("zh"),
            feat_index,
            first_dev,
            lax.axis_index("x"),
        ]
    ).astype(jnp.int32)
    schur, factor, reduced = gram_schur(count, at, gathered, near, far, inv, moments)
    return (schur, factor, reduced[0])


def solution(mesh):
    fine = Mesh(mesh.devices.reshape(4, 2, 4, 4, 2), ("x", "zh", "y", "zl", "core"))
    return jax.shard_map(
        per_device,
        mesh=fine,
        in_specs=(P(SAMP, None), P(None, FEAT), P(FEAT), P(FEAT), P(SAMP), P(SAMP), P()),
        out_specs=(P(SAMP, FEAT), P(SAMP, None), P(FEAT)),
        check_vma=False,
    )
```

```python
import jax
import jax.numpy as jnp
from jax import lax
from jax.experimental import pallas as pl
from jax.experimental.pallas import tpu as pltpu
from jax.sharding import Mesh
from jax.sharding import PartitionSpec as P

PANEL = 512
ridge = 0.1
f32 = jnp.float32
bf16 = jnp.bfloat16
HIGHEST = lax.Precision.HIGHEST

SAMP = ("x", "zh")
FEAT = ("y", "zl", "core")

SINE = (
    -8.885765875337938,
    58.46599556065702,
    -115.4071939365197,
    108.47536728137668,
    -59.39695452559278,
    20.275610646954046,
)


def cosine(x):
    turns = x * 0.15915494309189535
    s = jnp.abs(turns - jnp.round(turns)) - 0.25
    u = s * s
    p = SINE[5]
    for c in SINE[4::-1]:
        p = p * u + c
    return s * p


def dot(left, right, dims, **kw):
    return lax.dot_general(left, right, (dims, ((), ())), preferred_element_type=f32, **kw)


NN = ((1,), (0,))
NT = ((1,), (1,))


def invert_body(a_ref, out_ref, work, diag):
    n = a_ref.shape[0]
    nb = 128
    work[:, :n] = a_ref[...]
    row = lax.broadcasted_iota(jnp.int32, (n, n), 0)
    col = lax.broadcasted_iota(jnp.int32, (n, n), 1)
    work[:, n:] = (row == col).astype(f32)
    sub = lax.broadcasted_iota(jnp.int32, (8, nb), 0)
    lane = lax.broadcasted_iota(jnp.int32, (8, nb), 1)
    eye = (
        lax.broadcasted_iota(jnp.int32, (nb, nb), 0) == lax.broadcasted_iota(jnp.int32, (nb, nb), 1)
    ).astype(f32)
    for lo in range(0, n, nb):
        hi = lo + nb
        diag[:, :nb] = work[lo:hi, lo:hi]
        diag[:, nb:] = eye

        def slab(k, carry):
            q = pl.multiple_of(8 * k, 8)
            ra = diag[pl.ds(q, 8), :nb]
            rb = diag[pl.ds(q, 8), nb:]
            cols = [
                jnp.broadcast_to(
                    jnp.sum(jnp.where(lane == q + c, ra, 0.0), axis=1, keepdims=True), (8, nb)
                )
                for c in range(8)
            ]
            pivots = jnp.ones((8, nb), f32)
            for c in range(8):
                d = jnp.broadcast_to(cols[c][c : c + 1, :], (8, nb))
                pivots = jnp.where(sub == c, d, pivots)
                mult = jnp.where(sub > c, cols[c] / d, 0.0)
                for e in range(c + 1, 8):
                    cols[e] = cols[e] - mult * jnp.broadcast_to(cols[e][c : c + 1, :], (8, nb))
                ra = ra - mult * jnp.broadcast_to(ra[c : c + 1, :], (8, nb))
                rb = rb - mult * jnp.broadcast_to(rb[c : c + 1, :], (8, nb))
            scale = lax.rsqrt(pivots)
            ra = ra * scale
            rb = rb * scale
            diag[pl.ds(q, 8), nb:] = rb
            low = jnp.where(lane >= q + 8, ra, 0.0)
            update = dot(low, jnp.concatenate([low, rb], 1), ((0,), (0,)), precision=HIGHEST)
            diag[...] = diag[...] - update
            return carry

        lax.fori_loop(0, nb // 8, slab, 0)
        upper = dot(diag[:, nb:], work[lo:hi, hi : n + hi], ((1,), (0,)), precision=HIGHEST)
        rest = n - hi
        out_ref[lo:hi, :hi] = upper[:, rest:]
        if rest:
            work[hi:, hi : n + hi] = work[hi:, hi : n + hi] - dot(
                upper[:, :rest], upper, ((0,), (0,)), precision=HIGHEST
            )
            out_ref[lo:hi, hi:] = jnp.zeros((nb, rest), f32)


def inverse_factor(pivot):
    n = pivot.shape[0]
    return pl.pallas_call(
        invert_body,
        out_shape=jax.ShapeDtypeStruct((n, n), f32),
        scratch_shapes=[pltpu.VMEM((n, 2 * n), f32), pltpu.VMEM((128, 256), f32)],
        compiler_params=pltpu.CompilerParams(vmem_limit_bytes=16 << 20),
        cost_estimate=pl.CostEstimate(flops=30 * 10**9, bytes_accessed=2 << 20, transcendentals=0),
        name="inverse_factor",
    )(pivot)


def gram_body(
    count, at_ref, all_ref, near_ref, far0, far1, far2, far3, inv_ref, mom,
    schur_ref, factor_ref, red_ref, own, panel, mine_ref,
):
    step = pl.program_id(0)
    imps = near_ref.shape[1]
    width = near_ref.shape[2]
    feat = all_ref.shape[0]
    piece = imps // feat
    rows = panel.shape[1]
    row_blocks = rows // width
    blocks = row_blocks + PANEL // width

    @pl.when(step == 0)
    def _():
        own[...] = jnp.zeros_like(own)
        panel[...] = jnp.zeros_like(panel)

    zh = at_ref[3]
    mine_ref[zh] = near_ref[0].T
    for k, ref in enumerate((far0, far1, far2, far3)):

        @pl.when(((step - at_ref[6]) & 3) == k)
        def _():
            mine_ref[1 - zh] = ref[...].T

    def block(half, b):
        return all_ref[:, half, b * piece : (b + 1) * piece, :].reshape(imps, width)

    elim = [
        jnp.concatenate([block(half, b) for b in range(row_blocks, blocks)], axis=1)
        for half in range(2)
    ]
    left = [jnp.concatenate([mine_ref[half], elim[half].T], axis=0) for half in range(2)]
    both = jnp.concatenate(left, axis=1)
    for b in range(row_blocks):
        at = slice(b * width, (b + 1) * width)
        sums = dot(both, jnp.concatenate([block(0, b), block(1, b)], axis=0), NN)
        own[:, at] += sums[:width]
        panel[:, at] += sums[width:]
    own[:, rows:] += dot(mine_ref[0], elim[0], NN) + dot(mine_ref[1], elim[1], NN)

    @pl.when(step == pl.num_programs(0) - 1)
    def _():
        row0, col0, first = at_ref[0], at_ref[1], at_ref[2]
        scale = 1.0 / count

        def diagonal(shape, r0, c0):
            r = r0 + lax.broadcasted_iota(jnp.int32, shape, 0)
            c = c0 + lax.broadcasted_iota(jnp.int32, shape, 1)
            return jnp.where(r == c, ridge, 0.0)

        inv = inv_ref[...].T
        part = PANEL // 2

        def solve(a):
            return jnp.concatenate(
                [
                    dot(a[:, :part], inv[:part, :part], NN, precision=HIGHEST),
                    dot(a, inv[:, part:], NN, precision=HIGHEST),
                ],
                axis=1,
            )

        cross = own[:, rows:] * scale + diagonal((width, PANEL), col0, first)
        cross = solve(cross)
        cross_t = cross.T
        for lo in range(0, rows, width):
            at = slice(lo, lo + width)
            cols = panel[:, at].T * scale + diagonal((width, PANEL), row0 + lo, first)
            factor = solve(cols)
            factor_ref[at, :] = factor
            gram = own[:, at].T * scale + diagonal((width, width), row0 + lo, col0)
            schur_ref[at, :] = gram - dot(factor, cross_t, NN, precision=HIGHEST)
        own_dev = at_ref[4]
        first_dev = at_ref[5]
        picked = [mom[pl.ds(first_dev + k, 1), :] for k in range(PANEL // width)]
        elim = jnp.broadcast_to(jnp.concatenate(picked, axis=1), (8, PANEL))
        solved = dot(elim, inv_ref[...], NT, precision=HIGHEST)
        taken = dot(solved, cross, NT, precision=HIGHEST)
        reduced = mom[pl.ds(own_dev, 1), :] - taken[:1]
        red_ref[...] = reduced * (count**0.5)


def gram_schur(count, at, gathered, near, far, inv, moments):
    feat, samp, held, width = gathered.shape
    imps = near.shape[1]
    rows = width * feat // samp
    fixed = lambda i, at_ref: (0, 0)
    whole = list(far) + [inv, moments]
    return pl.pallas_call(
        lambda *refs: gram_body(count, *refs),
        out_shape=(
            jax.ShapeDtypeStruct((rows, width), f32),
            jax.ShapeDtypeStruct((rows, PANEL), f32),
            jax.ShapeDtypeStruct((1, width), f32),
        ),
        grid_spec=pltpu.PrefetchScalarGridSpec(
            num_scalar_prefetch=1,
            grid=(samp // 2,),
            in_specs=[
                pl.BlockSpec((feat, 2, held, width), lambda i, at_ref: (0, i, 0, 0)),
                pl.BlockSpec((1, imps, width), lambda i, at_ref: (i, 0, 0)),
            ]
            + [pl.BlockSpec(a.shape, fixed) for a in whole],
            out_specs=[
                pl.BlockSpec((rows, width), fixed),
                pl.BlockSpec((rows, PANEL), fixed),
                pl.BlockSpec((1, width), fixed),
            ],
            scratch_shapes=[
                pltpu.VMEM((width, rows + PANEL), f32),
                pltpu.VMEM((PANEL, rows), f32),
                pltpu.VMEM((2, width, imps), bf16),
            ],
        ),
        compiler_params=pltpu.CompilerParams(vmem_limit_bytes=50 << 20),
        cost_estimate=pl.CostEstimate(flops=20 * 10**9, bytes_accessed=30 << 20, transcendentals=0),
        name="gram_schur",
    )(at, gathered, near, *whole)


def per_device(embeddings, frequencies, phases, treat_freq, treatment, flips, panel):
    imps = embeddings.shape[0]
    width = frequencies.shape[1]
    samp = lax.axis_size(SAMP)
    feat = lax.axis_size(FEAT)
    samp_index = lax.axis_index(SAMP)
    feat_index = lax.axis_index(FEAT)
    count = imps * samp
    rows = width * feat // samp
    piece = imps // feat
    elim = PANEL // width

    project = jnp.dot(embeddings, frequencies, preferred_element_type=f32)
    treated = treatment.astype(f32)
    flipped = flips.astype(f32)
    counter = treated + flipped - 2.0 * treated * flipped
    base = project + phases[None, :]
    observed = cosine(base + treated[:, None] * treat_freq[None, :])
    counterfactual = cosine(base + counter[:, None] * treat_freq[None, :])
    moment_part = jnp.sum(counterfactual - observed, axis=0)
    feature = observed.astype(bf16)

    near = lax.all_gather(feature, "x")

    shares = lax.all_to_all(
        feature.reshape(feat, piece, width), FEAT, split_axis=0, concat_axis=0, tiled=True
    )
    first_dev = panel[0] * elim
    picked = lax.dynamic_slice_in_dim(shares, first_dev, elim, 0).reshape(1, elim * piece, width)
    send = jnp.concatenate(
        [
            shares.reshape(samp, feat // samp * piece, width),
            jnp.broadcast_to(picked, (samp, elim * piece, width)),
        ],
        axis=1,
    )
    share = lax.all_to_all(send, SAMP, split_axis=0, concat_axis=0, tiled=True)
    share, near = lax.optimization_barrier((share, near))
    gathered = lax.all_gather(share, FEAT)

    share, feature, moment_part = lax.optimization_barrier((share, feature, moment_part))
    swapped = lax.ppermute(feature, "zh", [(0, 1), (1, 0)])
    skip = feat // samp * piece
    mine = jnp.concatenate(
        [
            share[:, skip + k * piece : skip + (k + 1) * piece, :].reshape(samp * piece, width)
            for k in range(elim)
        ],
        axis=1,
    )
    xs = lax.axis_size("x")
    part_rows = PANEL // xs
    left = lax.dynamic_slice_in_dim(mine, lax.axis_index("x") * part_rows, part_rows, 1)
    partial = dot(left, mine, ((0,), (0,))).reshape(feat, part_rows // feat * PANEL)
    slabs = lax.all_to_all(partial, FEAT, split_axis=0, concat_axis=0, tiled=True)
    held = jnp.concatenate([jnp.sum(slabs, axis=0), moment_part])[None]
    held = lax.all_gather(held, ("zl", "core"), axis=0, tiled=True)
    held = lax.all_gather(held, "y", axis=0, tiled=True)
    cut = part_rows // feat * PANEL
    other = lax.ppermute(held[:, cut:], "zh", [(0, 1), (1, 0)])
    held = jnp.concatenate([held[:, :cut], held[:, cut:] + other], axis=1)
    table = lax.all_to_all(
        jnp.broadcast_to(held[None], (xs,) + held.shape), "x", split_axis=0, concat_axis=0, tiled=True
    )
    far = [swapped] + [
        lax.ppermute(swapped, "x", [(i, (i - r) % xs) for i in range(xs)]) for r in range(1, xs)
    ]
    pivot = table[..., :cut].reshape(PANEL, PANEL) / count
    moments = jnp.sum(table[..., cut:].reshape(xs, feat, width), axis=0) / count
    inv = inverse_factor(pivot + ridge * jnp.eye(PANEL, dtype=f32))

    at = jnp.stack(
        [
            samp_index * rows,
            feat_index * width,
            panel[0] * PANEL,
            lax.axis_index("zh"),
            feat_index,
            first_dev,
            lax.axis_index("x"),
        ]
    ).astype(jnp.int32)
    schur, factor, reduced = gram_schur(count, at, gathered, near, far, inv, moments)
    return (schur, factor, reduced[0])


def solution(mesh):
    fine = Mesh(mesh.devices.reshape(4, 2, 4, 4, 2), ("x", "zh", "y", "zl", "core"))
    return jax.shard_map(
        per_device,
        mesh=fine,
        in_specs=(P(SAMP, None), P(None, FEAT), P(FEAT), P(FEAT), P(SAMP), P(SAMP), P()),
        out_specs=(P(SAMP, FEAT), P(SAMP, None), P(FEAT)),
        check_vma=False,
    )
```
